32 devices in a mesh: fsdp: 32 (over z, y, x, core).
Axes of the slice: x: 2, y: 2, z: 4, core: 2. Of those that a mesh axis runs over, the one named last changes fastest.
Arguments:
- latents: bfloat16 [224, 256, 384], P('fsdp'), may hold values from -6 to 6
- cond: bfloat16 [224, 384], P('fsdp'), may hold values from -6 to 6
- live_counts: int32 [32], P('fsdp'), may hold values from 1 to 7, 149 in all
- ada_weight: bfloat16 [2, 384, 2304], P(None, None, 'fsdp'), may hold values from -0.3125 to 0.3125
- attn_weight: bfloat16 [2, 384, 1536], P(None, None, 'fsdp'), may hold values from -1 to 1
- mlp_in: bfloat16 [2, 384, 1536], P(None, None, 'fsdp'), may hold values from -0.3125 to 0.3125
- mlp_out: bfloat16 [2, 1536, 384], P(None, 'fsdp'), may hold values from -0.15625 to 0.15625
- bias_all: bfloat16 [2, 5376], P(None, 'fsdp'), may hold values from -3 to 3
- cotangent: bfloat16 [224, 256, 384], P('fsdp'), may hold values from -6 to 6
Outputs:
- activations: bfloat16 [224, 256, 384], P('fsdp')
- grad_latents: float32 [224, 256, 384], P('fsdp')
- grad_cond: float32 [224, 384], P('fsdp')
- grad_ada_weight: float32 [2, 384, 2304], P(None, None, 'fsdp')
- grad_attn_weight: float32 [2, 384, 1536], P(None, None, 'fsdp')
- grad_mlp_in: float32 [2, 384, 1536], P(None, None, 'fsdp')
- grad_mlp_out: float32 [2, 1536, 384], P(None, 'fsdp')
- grad_bias: float32 [2, 5376], P(None, 'fsdp')
The draws below stay inside these ranges and needn't reach their ends.
Inputs may be any that keep to these rules, and one draw needn't show every extreme that they name: `live_counts`: the live latents of a device fill its first slots; the counts sum to 149.
All inputs are finite; a program needn't handle non-finite values.
Results may differ from the reference program's by a relative error of at most 0.013.
Values may be sent and summed in bfloat16 or wider, within the bound.
No kernel may reach another device: no remote copies, remote signals or barrier semaphores. Data moves between devices by JAX's collectives and lax.ppermute only.
A program may use at most 256 MiB of HBM per device.

```python
import math
import jax
import jax.numpy as jnp
import numpy as np
from jax import lax

D = 384
HEADS = 6
HEAD_DIM = 64
FF = 1536
SEQ = 256
LAYERS = 2
LAT_DEV = 7
SLOTS = 224
LIVE = 149
BIAS = 5376
N_FSDP = 32


def drawn_field(key, shape, scale, bound):
    spread = jax.random.normal(key, shape, jnp.float32)
    return jnp.clip(spread * scale, -bound, bound).astype(jnp.bfloat16)


def draw_latents(key, part):
    return drawn_field(jax.random.fold_in(key, 11), (SLOTS, SEQ, D), 1.0, 6.0)


def draw_cond(key, part):
    return drawn_field(jax.random.fold_in(key, 12), (SLOTS, D), 1.0, 6.0)


def draw_cotangent(key, part):
    return drawn_field(jax.random.fold_in(key, 13), (SLOTS, SEQ, D), 1.0, 6.0)


def draw_bias_all(key, part):
    return drawn_field(jax.random.fold_in(key, 14), (LAYERS, BIAS), 0.5, 3.0)


def draw_attn_weight(key, part):
    base = jnp.clip(jax.random.normal(key, (LAYERS, D, 4 * D), jnp.float32), -6.0, 6.0)
    column = jnp.arange(4 * D)
    factor = jnp.where(column >= 3 * D, 4.0, 1.0).astype(jnp.float32)
    return jnp.clip(base * factor * D ** (-0.5), -1.0, 1.0).astype(jnp.bfloat16)


def block_scale(key, extent, cuts, least, top_value):
    def one(dim, blocks):
        draws = jax.random.uniform(jax.random.fold_in(jax.random.fold_in(key, 6), dim), (blocks,), jnp.float32, least / len(cuts), top_value / len(cuts))
        return jnp.repeat(jnp.exp(draws), extent[dim] // blocks).reshape((-1,) + (1,) * (len(extent) - dim - 1))

    level = one(*cuts[0])
    for cut in cuts[1:]:
        level = level * one(*cut)
    return level


def length_profile(number_of, total, most, lean):
    portions = [(1 << 20) // math.isqrt(grade ** lean) + 1 for grade in range(2, number_of + 1)]
    rest, counts = total - most - (number_of - 1), [1] * (number_of - 1)
    while rest > 0:
        free = [i for i in range(number_of - 1) if counts[i] < most]
        mass, budget = sum([portions[i] for i in free]), rest
        for i in free:
            extra = min(most - counts[i], max(1, budget * portions[i] // mass), rest)
            counts[i] = counts[i] + extra
            rest = rest - extra
    return np.array([most] + counts)


def ragged_sizes(stream_key, number_of, total, reach, slope):
    if number_of == 2:
        one = jax.random.randint(stream_key, (), max(1, total - reach), min(reach, total - 1) + 1)
        return jnp.stack([one, total - one])
    tallies = jnp.asarray(length_profile(number_of, total, reach, slope), jnp.int32)
    pairs = (number_of - 1) // 2
    giver, taker = tallies[1:1 + 2 * pairs:2], tallies[2:2 + 2 * pairs:2]
    room = jnp.minimum(giver - 1, reach - taker)
    shifted = jax.random.randint(jax.random.fold_in(stream_key, 1), (pairs,), 0, 1 << 20) % (room + 1)
    tallies = tallies.at[1:1 + 2 * pairs:2].set(giver - shifted).at[2:2 + 2 * pairs:2].set(taker + shifted)
    return tallies[jax.random.permutation(jax.random.fold_in(stream_key, 2), number_of)]


def scatter_about(key, shape, deviation, most, split=(), kind=jnp.bfloat16):
    factor_of = block_scale(key, shape, split, -0.22, 0.18) if split else 1.0
    entries = jax.random.normal(key, shape, jnp.float32) * deviation * factor_of
    return jnp.minimum(jnp.maximum(entries, -most), most).astype(kind)


def setup_inputs(seed: int = 0) -> dict:
    key_of = jax.random.split(jax.random.key(seed), 10)
    return {
        "latents": draw_latents(jax.random.fold_in(key_of[9], 71), 0),
        "cond": draw_cond(jax.random.fold_in(key_of[9], 71), 0),
        "live_counts": ragged_sizes(key_of[2], N_FSDP, LIVE, LAT_DEV, 2).astype(jnp.int32),
        "ada_weight": scatter_about(key_of[3], (LAYERS, D, 6 * D), D ** -0.5, 0.3125, ((2, 32),)),
        "attn_weight": draw_attn_weight(jax.random.fold_in(key_of[9], 71), 0),
        "mlp_in": scatter_about(key_of[5], (LAYERS, D, FF), D ** -0.5, 0.3125, ((2, 32),)),
        "mlp_out": scatter_about(key_of[6], (LAYERS, FF, D), FF ** -0.5, 0.15625, ((1, 32),)),
        "bias_all": draw_bias_all(jax.random.fold_in(key_of[9], 71), 0),
        "cotangent": draw_cotangent(jax.random.fold_in(key_of[9], 71), 0),
    }


@jax.custom_vjp
def low(v):
    return lax.optimization_barrier(v.astype(jnp.bfloat16)).astype(jnp.float32)

@jax.custom_vjp
def low_back(v):
    return v

def low_keep(v):
    return (low(v), None)

def low_pass(kept, grad):
    return (grad,)

def back_keep(v):
    return (v, None)

def back_low(kept, grad):
    return (low(grad),)
low.defvjp(low_keep, low_pass)
low_back.defvjp(back_keep, back_low)

def silu_value(v):
    return v / (1.0 + jnp.exp(-v))

def gelu_value(v):
    return 0.5 * v * (1.0 + jnp.tanh(0.7978845608028654 * (v + 0.044715 * v * v * v)))

def layer_norm(v):
    centre = v - lax.optimization_barrier(jnp.mean(v, -1, keepdims=True))
    spread = lax.optimization_barrier(jnp.mean(centre * centre, -1, keepdims=True))
    return centre * lax.rsqrt(spread + 1e-06)

def one_layer(residual, cond_low, weights):
    ada_full, attn_full, inner_weight, outer_weight, bias_full = weights
    highest = lax.Precision.HIGHEST
    modulate = low_back(jnp.dot(cond_low, ada_full, precision=highest) + bias_full[:6 * D])
    pieces = [modulate[:, None, piece_index * D:(piece_index + 1) * D] for piece_index in range(6)]
    shift_one, scale_one, gate_one, shift_two, scale_two, gate_two = pieces
    hidden_one = low(layer_norm(residual) * (1.0 + scale_one) + shift_one)
    project = jnp.einsum('gnd,de->gne', hidden_one, attn_full[:, :3 * D], precision=highest)
    query_matrix = low(low_back(project[..., :D] + bias_full[6 * D:7 * D]))
    key_matrix = low(low_back(project[..., D:2 * D]))
    value_matrix = low(low_back(project[..., 2 * D:3 * D] + bias_full[7 * D:8 * D]))
    head_shape = residual.shape[:2] + (HEADS, HEAD_DIM)
    scores = low_back(jnp.einsum('gnhd,gmhd->ghnm', query_matrix.reshape(head_shape), key_matrix.reshape(head_shape), precision=highest) * HEAD_DIM ** (-0.5))
    row_max = lax.optimization_barrier(jnp.max(scores, -1, keepdims=True))
    expo = jnp.exp(scores - row_max)
    softmax_weights = expo / lax.optimization_barrier(jnp.sum(expo, -1, keepdims=True))
    attended = jnp.einsum('ghnm,gmhd->gnhd', low(softmax_weights), value_matrix.reshape(head_shape), precision=highest)
    attended = low(low_back(attended.reshape(residual.shape)))
    branch_one = low_back(jnp.einsum('gnd,de->gne', attended, attn_full[:, 3 * D:], precision=highest) + bias_full[8 * D:9 * D])
    middle = residual + gate_one * branch_one
    hidden_two = low(layer_norm(middle) * (1.0 + scale_two) + shift_two)
    inner_pre = low_back(jnp.einsum('gnd,df->gnf', hidden_two, inner_weight, precision=highest) + bias_full[10 * D:])
    activated = low(gelu_value(inner_pre))
    branch_two = low_back(jnp.einsum('gnf,fd->gnd', activated, outer_weight, precision=highest) + bias_full[9 * D:10 * D])
    return middle + gate_two * branch_two

def forward_all(block_latents, block_cond, params):
    cond_low = low(silu_value(block_cond))
    residual = block_latents
    for layer_index in range(LAYERS):
        residual = one_layer(residual, cond_low, tuple((array[layer_index] for array in params)))
    return residual

def reference(latents, cond, live_counts, ada_weight, attn_weight, mlp_in, mlp_out, bias_all, cotangent):
    slot_index = jnp.arange(SLOTS, dtype=jnp.int32)
    owner = slot_index // LAT_DEV
    live_mask = (slot_index % LAT_DEV < live_counts[owner]).astype(jnp.float32)
    params = tuple((array.astype(jnp.float32) for array in (ada_weight, attn_weight, mlp_in, mlp_out, bias_all)))
    bundle = 16
    count_groups = SLOTS // bundle
    inputs = (latents.astype(jnp.float32).reshape(count_groups, bundle, SEQ, D), cond.astype(jnp.float32).reshape(count_groups, bundle, D), cotangent.astype(jnp.float32).reshape(count_groups, bundle, SEQ, D), live_mask.reshape(count_groups, bundle))

    def group_step(totals, group_items):
        block_latents, block_cond, block_cotangent, block_live = group_items
        result, pullback = jax.vjp(forward_all, block_latents, block_cond, params)
        grad_block, grad_cond_block, grad_params = pullback(block_cotangent * block_live[:, None, None])
        totals = jax.tree.map(lambda left, right: left + right, totals, grad_params)
        return (totals, ((result * block_live[:, None, None]).astype(jnp.bfloat16), grad_block, grad_cond_block))
    totals, outputs = lax.scan(group_step, jax.tree.map(jnp.zeros_like, params), inputs)
    acts, grad_rows, grad_conds = outputs
    return (acts.reshape(SLOTS, SEQ, D), grad_rows.reshape(SLOTS, SEQ, D), grad_conds.reshape(SLOTS, D), totals[0], totals[1], totals[2], totals[3], totals[4])
```

```python
import jax
import jax.numpy as jnp
from jax import lax
from jax.experimental import pallas as pl
from jax.experimental.pallas import tpu as pltpu
from jax.sharding import PartitionSpec as P

HEADS = 6
D = 384
F = 1536
S = 256
BF = jnp.bfloat16
F32 = jnp.float32
SPLIT = 32
BLOCKS = 32
ROWS = 144
AXIS = "fsdp"


def dot_nn(a, b):
    return lax.dot_general(a, b, (((1,), (0,)), ((), ())), preferred_element_type=F32)


def dot_nt(a, b):
    return lax.dot_general(a, b, (((1,), (1,)), ((), ())), preferred_element_type=F32)


def silu_value(v):
    return v / (1.0 + jnp.exp(-v))


def silu_slope(v):
    sigmoid = 1.0 / (1.0 + jnp.exp(-v))
    return sigmoid * (1.0 + v * (1.0 - sigmoid))


def layer_norm(v):
    centre = v - jnp.mean(v, -1, keepdims=True)
    spread = jnp.mean(centre * centre, -1, keepdims=True)
    inverse = lax.rsqrt(spread + 1e-06)
    return centre * inverse, inverse


def norm_back(e, y, inverse):
    first = jnp.mean(e, -1, keepdims=True)
    second = jnp.mean(e * y, -1, keepdims=True)
    return inverse * (e - first - y * second)


def gelu_parts(u):
    square = u * u
    tanh = jnp.tanh(u * (0.7978845608028654 + (0.7978845608028654 * 0.044715) * square))
    return square, tanh


def gelu_value(u):
    _, tanh = gelu_parts(u)
    half = 0.5 * u
    return half + half * tanh


def gelu_both(u):
    square, tanh = gelu_parts(u)
    half = 0.5 * u
    value = half + half * tanh
    inner = 0.7978845608028654 + (3 * 0.7978845608028654 * 0.044715) * square
    slope = 0.5 + 0.5 * tanh + half * (1.0 - tanh * tanh) * inner
    return value, slope


def stack_heads(pair):
    lane = lax.broadcasted_iota(jnp.int32, pair.shape, 1)
    zero = jnp.zeros_like(pair)
    return jnp.concatenate([jnp.where(lane < 64, pair, zero), jnp.where(lane >= 64, pair, zero)], axis=0)


def attn_weight_of(wv, low, high):
    return wv[low:high, 0:48, :].reshape((high - low) * 48, D)


def inner_chunk(wv, c, base):
    return wv[16 * c : 16 * c + 16, base : base + 48, :].reshape(768, D)


def tile_of(modulation, k):
    return modulation[:, k * D : (k + 1) * D]


def forward_body(r, mod, bias, wv, keep):
    qkv_ref, prob_ref, att_ref, br1_ref, mid_ref, inn_ref, br2_ref = keep
    normed, _ = layer_norm(r)
    hidden = (normed * (1.0 + tile_of(mod, 1)) + tile_of(mod, 0)).astype(BF)
    per = D // 48
    for part, at in ((0, 0), (1, None), (2, 1)):
        project = dot_nt(hidden, attn_weight_of(wv, part * per, part * per + per))
        if at is not None:
            project = project + tile_of(bias, at)
        qkv_ref[:, part * D : (part + 1) * D] = project.astype(BF)
    for pair in range(HEADS // 2):
        lo = pair * 128
        query = qkv_ref[:, lo : lo + 128] * jnp.asarray(0.125, BF)
        key = stack_heads(qkv_ref[:, D + lo : D + lo + 128])
        value = stack_heads(qkv_ref[:, 2 * D + lo : 2 * D + lo + 128])
        scores = dot_nt(query, key)
        for h in range(2):
            part = scores[:, h * S : (h + 1) * S]
            expo = jnp.exp(part - jnp.max(part, -1, keepdims=True))
            total = jnp.sum(expo, -1, keepdims=True)
            prob_ref[:, (2 * pair + h) * S : (2 * pair + h + 1) * S] = (expo * (1.0 / total)).astype(BF)
        probs = prob_ref[:, 2 * pair * S : (2 * pair + 2) * S]
        att_ref[:, lo : lo + 128] = dot_nn(probs, value).astype(BF)
    branch = dot_nt(att_ref[...], attn_weight_of(wv, 3 * per, 4 * per)) + tile_of(bias, 2)
    br1_ref[...] = branch
    middle = r + tile_of(mod, 2) * branch
    mid_ref[...] = middle
    normed, _ = layer_norm(middle)
    hidden = (normed * (1.0 + tile_of(mod, 4)) + tile_of(mod, 3)).astype(BF)
    branch = tile_of(bias, 3)
    for c in range(2):
        inner = dot_nt(hidden, inner_chunk(wv, c, 48)) + bias[:, 4 * D + 768 * c : 4 * D + 768 * (c + 1)]
        inn_ref[:, 768 * c : 768 * (c + 1)] = inner
        branch = branch + dot_nn(gelu_value(inner).astype(BF), inner_chunk(wv, c, 96))
    br2_ref[...] = branch
    return middle + tile_of(mod, 5) * branch


def column_sum(v):
    return jnp.sum(v, axis=0, keepdims=True)


def backward_body(g, r, mod, wv, keep, acc, dbias_ref, dmod_ref, row, dqkv_ref):
    qkv_ref, prob_ref, att_ref, br1_ref, mid_ref, inn_ref, br2_ref = keep
    acc_attn, acc_in, acc_out = acc
    per = D // 48

    def put(k, v):
        dmod_ref[pl.ds(row, 1), k * D : (k + 1) * D] = v

    def bias_add(lo, v):
        dbias_ref[:, lo : lo + v.shape[1]] += v

    d_br2 = (tile_of(mod, 5) * g).astype(BF)
    put(5, column_sum(g * br2_ref[...]))
    bias_add(3 * D, column_sum(d_br2.astype(F32)))
    d_br2_t = d_br2.T
    normed, inverse = layer_norm(mid_ref[...])
    scale = 1.0 + tile_of(mod, 4)
    hidden_t = (normed * scale + tile_of(mod, 3)).astype(BF).T
    d_hidden = None
    for c in range(2):
        cols = slice(768 * c, 768 * (c + 1))
        act, slope = gelu_both(inn_ref[:, cols])
        acc_out[:, cols] += dot_nn(d_br2_t, act.astype(BF))
        d_inner = (dot_nt(d_br2, inner_chunk(wv, c, 96)) * slope).astype(BF)
        bias_add(4 * D + 768 * c, column_sum(d_inner.astype(F32)))
        acc_in[:, cols] += dot_nn(hidden_t, d_inner)
        part = dot_nn(d_inner, inner_chunk(wv, c, 48))
        d_hidden = part if d_hidden is None else d_hidden + part
    put(4, column_sum(d_hidden * normed))
    put(3, column_sum(d_hidden))
    d_mid = g + norm_back(d_hidden * scale, normed, inverse)
    d_br1 = (tile_of(mod, 2) * d_mid).astype(BF)
    put(2, column_sum(d_mid * br1_ref[...]))
    bias_add(2 * D, column_sum(d_br1.astype(F32)))
    acc_attn[:, 3 * D : 4 * D] += dot_nn(att_ref[...].T, d_br1)
    d_att = dot_nn(d_br1, attn_weight_of(wv, 3 * per, 4 * per)).astype(BF)
    for pair in range(HEADS // 2):
        lo = pair * 128
        query = qkv_ref[:, lo : lo + 128] * jnp.asarray(0.125, BF)
        key = stack_heads(qkv_ref[:, D + lo : D + lo + 128])
        value = stack_heads(qkv_ref[:, 2 * D + lo : 2 * D + lo + 128])
        d_out = d_att[:, lo : lo + 128]
        both = d_out.astype(F32) * att_ref[:, lo : lo + 128].astype(F32)
        lane = lax.broadcasted_iota(jnp.int32, both.shape, 1)
        d_probs = dot_nt(d_out, value)
        pieces = []
        probs = []
        for h in range(2):
            chosen = lane < 64 if h == 0 else lane >= 64
            delta = jnp.sum(jnp.where(chosen, both, 0.0), -1, keepdims=True)
            prob = prob_ref[:, (2 * pair + h) * S : (2 * pair + h + 1) * S]
            probs.append(prob)
            pieces.append((prob.astype(F32) * (d_probs[:, h * S : (h + 1) * S] - delta)).astype(BF))
        d_query = (dot_nn(jnp.concatenate(pieces, axis=1), key) * 0.125).astype(BF)
        d_scores = jnp.concatenate(pieces, axis=0)
        d_key = dot_nn(split_rows(query.T), d_scores).T.astype(BF)
        d_value = dot_nn(split_rows(d_out.T), jnp.concatenate(probs, axis=0)).T.astype(BF)
        dqkv_ref[:, lo : lo + 128] = d_query
        dqkv_ref[:, D + lo : D + lo + 128] = d_key
        dqkv_ref[:, 2 * D + lo : 2 * D + lo + 128] = d_value
        bias_add(lo, column_sum(d_query.astype(F32)))
        bias_add(D + lo, column_sum(d_value.astype(F32)))
    normed, inverse = layer_norm(r)
    scale = 1.0 + tile_of(mod, 1)
    hidden_t = (normed * scale + tile_of(mod, 0)).astype(BF).T
    d_hidden = None
    for part in range(3):
        cols = slice(part * D, (part + 1) * D)
        d_part = dqkv_ref[:, cols]
        acc_attn[:, cols] += dot_nn(hidden_t, d_part)
        term = dot_nn(d_part, attn_weight_of(wv, part * per, part * per + per))
        d_hidden = term if d_hidden is None else d_hidden + term
    put(1, column_sum(d_hidden * normed))
    put(0, column_sum(d_hidden))
    return d_mid + norm_back(d_hidden * scale, normed, inverse)


def split_rows(pair):
    sub = lax.broadcasted_iota(jnp.int32, pair.shape, 0)
    zero = jnp.zeros_like(pair)
    return jnp.concatenate([jnp.where(sub < 64, pair, zero), jnp.where(sub >= 64, pair, zero)], axis=1)


def fetch_weights(table, pieces, wv, sem):
    copies = []
    for ref, (masks, low, rows) in pieces:
        for k, mask in enumerate(masks):
            block = table[mask]
            copies.append(
                pltpu.make_async_copy(ref.at[k], wv.at[block, pl.ds(low, rows), :], sem.at[len(copies)])
            )
    for copy in copies:
        copy.start()
    for copy in copies:
        copy.wait()


def emit_grads(table, acc, stage, outs, orders, sem):
    for part, ref in enumerate(acc):
        for k in range(4):
            block = ref[:, k * D : (k + 1) * D].T.astype(BF)
            stage[8 * k : 8 * k + 8, 48 * part : 48 * part + 48, :] = block.reshape(8, 48, D)
    copies = []
    for ref, (masks, low, rows) in zip(outs, orders):
        for k, mask in enumerate(masks):
            copies.append(
                pltpu.make_async_copy(stage.at[table[mask], pl.ds(low, rows), :], ref.at[k], sem.at[len(copies)])
            )
    for copy in copies:
        copy.start()
    for copy in copies:
        copy.wait()


def saved_shapes():
    return [(3 * D, BF), (HEADS * S, BF), (D, BF), (D, F32), (D, F32), (F, F32), (D, F32)]


def run_forward(table, latents, mod, bias, pieces, layout):
    slots = latents.shape[0]
    count = len(pieces)

    def body(table_ref, lat_ref, mod_ref, bias_ref, *rest):
        piece_refs = rest[:count]
        keep = [ref.at[0] for ref in rest[count : count + 7]]
        out_ref, wv, sem = rest[count + 7 :]
        step = pl.program_id(0)

        @pl.when(step == 0)
        def _():
            fetch_weights(table_ref, list(zip(piece_refs, layout)), wv, sem)

        @pl.when(step < table_ref[BLOCKS])
        def _():
            out_ref[0] = forward_body(
                lat_ref[0].astype(F32), mod_ref[pl.ds(step, 1), :], bias_ref[...], wv, keep
            )

    clamp = lambda i, t: (jnp.minimum(i, t[BLOCKS] - 1), 0, 0)
    whole = lambda i, t: (0, 0)
    shapes = saved_shapes() + [(D, F32)]
    return pl.pallas_call(
        body,
        grid_spec=pltpu.PrefetchScalarGridSpec(
            num_scalar_prefetch=1,
            grid=(slots,),
            in_specs=[
                pl.BlockSpec((1, S, D), clamp),
                pl.BlockSpec(mod.shape, whole),
                pl.BlockSpec(bias.shape, whole),
            ]
            + [pl.BlockSpec(memory_space=pl.ANY)] * count,
            out_specs=[pl.BlockSpec((1, S, width), clamp) for width, _ in shapes],
            scratch_shapes=[
                pltpu.VMEM((32, ROWS, D), BF),
                pltpu.SemaphoreType.DMA((2 * BLOCKS,)),
            ],
        ),
        out_shape=[jax.ShapeDtypeStruct((slots, S, width), kind) for width, kind in shapes],
        cost_estimate=pl.CostEstimate(flops=slots * 1100000000, bytes_accessed=40000000, transcendentals=0),
        name="forward_zero",
    )(table, latents, mod, bias, *pieces)


def grad_outs():
    half = BLOCKS // 2
    shapes = [(half, SPLIT, D)] * 2 + [(half, ROWS - SPLIT, D)] * 2
    return [jax.ShapeDtypeStruct(shape, BF) for shape in shapes]


def run_middle(table, residual, cotangent, mod, bias, pieces, layout, orders):
    slots = residual.shape[0]
    count = len(pieces)

    def body(table_ref, res_ref, cot_ref, mod_ref, bias_ref, *rest):
        piece_refs = rest[:count]
        act_ref, g_ref, dmod_ref, dbias_ref = rest[count : count + 4]
        outs = rest[count + 4 : count + 8]
        wv, sem, a1, a2, a3, stage, dqkv = rest[count + 8 : count + 15]
        keep = rest[count + 15 :]
        acc = (a1, a2, a3)
        step = pl.program_id(0)

        @pl.when(step == 0)
        def _():
            fetch_weights(table_ref, list(zip(piece_refs, layout)), wv, sem)
            for ref in acc + (dbias_ref, dmod_ref):
                ref[...] = jnp.zeros_like(ref)

        @pl.when(step < table_ref[BLOCKS])
        def _():
            m = mod_ref[pl.ds(step, 1), :]
            r = res_ref[0]
            act_ref[0] = forward_body(r, m, bias_ref[...], wv, keep).astype(BF)
            g_ref[0] = backward_body(
                cot_ref[0].astype(F32), r, m, wv, keep, acc, dbias_ref, dmod_ref, step, dqkv
            )

        @pl.when(step >= table_ref[BLOCKS])
        def _():
            act_ref[0] = jnp.zeros((S, D), BF)

        @pl.when(step == slots - 1)
        def _():
            emit_grads(table_ref, acc, stage, outs, orders, sem)

    clamp = lambda i, t: (jnp.minimum(i, t[BLOCKS] - 1), 0, 0)
    each = lambda i, t: (i, 0, 0)
    whole = lambda i, t: (0, 0)
    any_spec = pl.BlockSpec(memory_space=pl.ANY)
    return pl.pallas_call(
        body,
        grid_spec=pltpu.PrefetchScalarGridSpec(
            num_scalar_prefetch=1,
            grid=(slots,),
            in_specs=[
                pl.BlockSpec((1, S, D), clamp),
                pl.BlockSpec((1, S, D), clamp),
                pl.BlockSpec(mod.shape, whole),
                pl.BlockSpec(bias.shape, whole),
            ]
            + [any_spec] * count,
            out_specs=[
                pl.BlockSpec((1, S, D), each),
                pl.BlockSpec((1, S, D), clamp),
                pl.BlockSpec((slots, 6 * D), whole),
                pl.BlockSpec((1, 8 * D), whole),
            ]
            + [any_spec] * 4,
            scratch_shapes=[
                pltpu.VMEM((32, ROWS, D), BF),
                pltpu.SemaphoreType.DMA((2 * BLOCKS,)),
                pltpu.VMEM((D, F), F32),
                pltpu.VMEM((D, F), F32),
                pltpu.VMEM((D, F), F32),
                pltpu.VMEM((32, ROWS, D), BF),
                pltpu.VMEM((S, 3 * D), BF),
            ]
            + [pltpu.VMEM((S, width), kind) for width, kind in saved_shapes()],
        ),
        out_shape=[
            jax.ShapeDtypeStruct((slots, S, D), BF),
            jax.ShapeDtypeStruct((slots, S, D), F32),
            jax.ShapeDtypeStruct((slots, 6 * D), F32),
            jax.ShapeDtypeStruct((1, 8 * D), F32),
        ]
        + grad_outs(),
        cost_estimate=pl.CostEstimate(flops=slots * 3300000000, bytes_accessed=20000000, transcendentals=0),
        name="middle_one",
    )(table, residual, cotangent, mod, bias, *pieces)


def run_backward(table, latents, upstream, mod, pieces, layout, saved, orders):
    slots = latents.shape[0]
    count = len(pieces)

    def body(table_ref, lat_ref, g_ref, mod_ref, *rest):
        keep = [ref.at[0] for ref in rest[:7]]
        piece_refs = rest[7 : 7 + count]
        rest = rest[7 + count :]
        out_ref, dmod_ref, dbias_ref = rest[:3]
        outs = rest[3:7]
        wv, sem, a1, a2, a3, stage, dqkv = rest[7:]
        acc = (a1, a2, a3)
        step = pl.program_id(0)

        @pl.when(step == 0)
        def _():
            fetch_weights(table_ref, list(zip(piece_refs, layout)), wv, sem)
            for ref in acc + (dbias_ref, dmod_ref):
                ref[...] = jnp.zeros_like(ref)

        @pl.when(step < table_ref[BLOCKS])
        def _():
            out_ref[0] = backward_body(
                g_ref[0],
                lat_ref[0].astype(F32),
                mod_ref[pl.ds(step, 1), :],
                wv,
                keep,
                acc,
                dbias_ref,
                dmod_ref,
                step,
                dqkv,
            )

        @pl.when(step >= table_ref[BLOCKS])
        def _():
            out_ref[0] = jnp.zeros((S, D), F32)

        @pl.when(step == slots - 1)
        def _():
            emit_grads(table_ref, acc, stage, outs, orders, sem)

    clamp = lambda i, t: (jnp.minimum(i, t[BLOCKS] - 1), 0, 0)
    each = lambda i, t: (i, 0, 0)
    whole = lambda i, t: (0, 0)
    any_spec = pl.BlockSpec(memory_space=pl.ANY)
    return pl.pallas_call(
        body,
        grid_spec=pltpu.PrefetchScalarGridSpec(
            num_scalar_prefetch=1,
            grid=(slots,),
            in_specs=[
                pl.BlockSpec((1, S, D), clamp),
                pl.BlockSpec((1, S, D), clamp),
                pl.BlockSpec(mod.shape, whole),
            ]
            + [pl.BlockSpec((1, S, width), clamp) for width, _ in saved_shapes()]
            + [any_spec] * count,
            out_specs=[
                pl.BlockSpec((1, S, D), each),
                pl.BlockSpec((slots, 6 * D), whole),
                pl.BlockSpec((1, 8 * D), whole),
            ]
            + [any_spec] * 4,
            scratch_shapes=[
                pltpu.VMEM((32, ROWS, D), BF),
                pltpu.SemaphoreType.DMA((2 * BLOCKS,)),
                pltpu.VMEM((D, F), F32),
                pltpu.VMEM((D, F), F32),
                pltpu.VMEM((D, F), F32),
                pltpu.VMEM((32, ROWS, D), BF),
                pltpu.VMEM((S, 3 * D), BF),
            ],
        ),
        out_shape=[
            jax.ShapeDtypeStruct((slots, S, D), F32),
            jax.ShapeDtypeStruct((slots, 6 * D), F32),
            jax.ShapeDtypeStruct((1, 8 * D), F32),
        ]
        + grad_outs(),
        cost_estimate=pl.CostEstimate(flops=slots * 2200000000, bytes_accessed=50000000, transcendentals=0),
        name="backward_zero",
    )(table, latents, upstream, mod, *saved, *pieces)


def permute(v, mask):
    size = lax.axis_size(AXIS)
    return lax.ppermute(v, AXIS, [(i, i ^ mask) for i in range(size)])


Z_MASKS = (0, 8, 16, 24)


def path_masks(first, second):
    order = [m for m in Z_MASKS]
    order = order + [m ^ second for m in order]
    return order + [m ^ first for m in order]


def gather_line(shard):
    return jnp.stack([shard] + [permute(shard, m) for m in Z_MASKS[1:]])


def gather_square(block, first, second):
    near = jnp.concatenate([block, permute(block, first)], axis=0)
    far = permute(near, second)
    return [near, far, permute(near, 1), permute(far, 1)]


def gather_block(wide, extra):
    wide_line = gather_line(wide)
    extra_line = gather_line(extra)
    one = gather_square(wide_line[:, :SPLIT], 2, 4)
    two = gather_square(wide_line[:, SPLIT:], 4, 2)
    extra_full = jnp.concatenate(gather_square(extra_line, 2, 4), axis=0)
    return one + two, extra_full


def gather_layout():
    layout = []
    for low, rows, masks in ((0, SPLIT, path_masks(4, 2)), (SPLIT, ROWS - SPLIT, path_masks(2, 4))):
        for core in (0, 1):
            for half in (0, 1):
                layout.append(([m ^ core for m in masks[8 * half : 8 * half + 8]], low, rows))
    return layout


def grad_orders():
    one, two = path_masks(4, 2), path_masks(2, 4)
    return [
        (one, 0, SPLIT),
        ([m ^ 1 for m in one], 0, SPLIT),
        (two, SPLIT, ROWS - SPLIT),
        ([m ^ 1 for m in two], SPLIT, ROWS - SPLIT),
    ]


def plain_layout():
    return [(list(range(BLOCKS)), 0, ROWS)]


def plain_orders():
    low, high = list(range(16)), list(range(16, 32))
    return [(low, 0, SPLIT), (high, 0, SPLIT), (low, SPLIT, ROWS - SPLIT), (high, SPLIT, ROWS - SPLIT)]


def added(*terms):
    total = terms[0].astype(F32)
    for term in terms[1:]:
        total = total + term.astype(F32)
    return total


def reduce_path(keep, send, first, second):
    total = added(keep, permute(send, 1)).astype(BF)
    total = added(total[:8], permute(total[8:], first)).astype(BF)
    total = added(total[:4], permute(total[4:], second)).astype(BF)
    return added(total[0], *[permute(total[k], Z_MASKS[k]) for k in range(1, 4)])


def flip_bits(v, me):
    lead = v.ndim - 2
    width = v.shape[-1]
    out = v
    for bit in range(5):
        stride = 1 << bit
        shaped = out.reshape(v.shape[:lead] + (BLOCKS // (2 * stride), 2, stride, width))
        out = jnp.where((me >> bit) & 1 == 1, jnp.flip(shaped, axis=lead + 1), shaped).reshape(v.shape)
    return out


def to_rank_order(v, me):
    lead = v.ndim - 2
    shaped = v.reshape(v.shape[:lead] + (2, 2, 2, 4, v.shape[-1]))
    axes = tuple(range(lead)) + (lead + 3, lead + 1, lead + 2, lead, lead + 4)
    return flip_bits(shaped.transpose(axes).reshape(v.shape), me)


def from_rank_order(v, me):
    lead = v.ndim - 2
    shaped = flip_bits(v, me).reshape(v.shape[:lead] + (4, 2, 2, 2, v.shape[-1]))
    axes = tuple(range(lead)) + (lead + 3, lead + 1, lead + 2, lead, lead + 4)
    return shaped.transpose(axes).reshape(v.shape)


def per_device(
    latents, cond, live_counts, ada_weight, attn_weight, mlp_in, mlp_out, bias_all, cotangent
):
    slots = latents.shape[0]
    layers = ada_weight.shape[0]
    fast = lax.axis_size(AXIS) == BLOCKS
    size = lax.axis_size(AXIS)
    me = lax.axis_index(AXIS)
    order = jnp.arange(BLOCKS, dtype=jnp.int32)
    if fast:
        order = order ^ me
    table = jnp.concatenate([order, live_counts.astype(jnp.int32)])
    cond_value = cond.astype(F32)
    cond_low = silu_value(cond_value).astype(BF)
    ada_rows = ada_weight.shape[2]
    attn_rows = attn_weight.shape[2]
    bias_count = bias_all.shape[1]
    gathered = []
    for layer in range(layers):
        wide = jnp.concatenate([attn_weight[layer].T, mlp_in[layer].T, mlp_out[layer]], axis=0)
        bias_row = jnp.pad(bias_all[layer], (0, D - bias_count))[None]
        if fast:
            extra = jnp.concatenate([ada_weight[layer].T, jnp.pad(bias_row, ((0, 7), (0, 0)))], axis=0)
            pieces, extra_full = gather_block(wide, extra)
            ada = extra_full[:, :ada_rows]
            bias = to_rank_order(extra_full[:, ada_rows, :bias_count], me).reshape(-1)
        else:
            packed = jnp.concatenate([wide, ada_weight[layer].T, bias_row], axis=0)
            full = lax.all_gather(packed, AXIS, axis=0, tiled=False)
            parts = [
                full[:, k * attn_rows : (k + 1) * attn_rows].reshape(BLOCKS, 48, D) for k in range(3)
            ]
            pieces = [jnp.concatenate(parts, axis=1)]
            ada = full[:, 3 * attn_rows : 3 * attn_rows + ada_rows].reshape(BLOCKS, -1, D)
            bias = full[:, 3 * attn_rows + ada_rows, :bias_count].reshape(-1)
        bias = bias.astype(F32)
        modulate = jnp.einsum("sd,jed->sje", cond_low, ada, preferred_element_type=F32)
        if fast:
            modulate = to_rank_order(modulate, me)
        modulate = modulate.reshape(slots, 6 * D) + bias[: 6 * D]
        gathered.append((pieces, ada, bias[None, 6 * D :], modulate))
    layout = gather_layout() if fast else plain_layout()
    orders = grad_orders() if fast else plain_orders()

    pieces, ada, bias, modulate = gathered[0]
    saved = run_forward(table, latents, modulate, bias, pieces, layout)
    residual = saved[7]
    results = [None, None]
    pieces, ada, bias, modulate = gathered[1]
    middle = run_middle(table, residual, cotangent, modulate, bias, pieces, layout, orders)
    output, upstream = middle[:2]
    results[1] = middle[2:]
    pieces, ada, bias, modulate = gathered[0]
    last = run_backward(table, latents, upstream, modulate, pieces, layout, saved[:7], orders)
    grad_latents = last[0]
    results[0] = last[1:]

    cond_grad = jnp.zeros(cond_value.shape, F32)
    shards = [None] * layers
    for layer in reversed(range(layers)):
        grad_modulate, grad_bias = results[layer][:2]
        wide_grads = results[layer][2:]
        ada = gathered[layer][1]
        grad_low = grad_modulate.astype(BF)
        bias_full = jnp.concatenate([jnp.sum(grad_low.astype(F32), axis=0), grad_bias[0]])
        grouped = grad_low.reshape(slots, BLOCKS, -1)
        if fast:
            grouped = from_rank_order(grouped, me)
        cond_grad = cond_grad + jnp.einsum("sje,jed->sd", grouped, ada, preferred_element_type=F32)
        ada_grad = jnp.einsum("sje,sd->jed", grouped, cond_low, preferred_element_type=F32)
        bias_rows = bias_full.reshape(size, bias_count)
        if fast:
            bias_rows = from_rank_order(bias_rows, me)
            tail = jnp.pad(bias_rows[:, None], ((0, 0), (0, 7), (0, D - bias_count)))
            extra = jnp.concatenate([ada_grad.astype(BF), tail.astype(BF)], axis=1)
            keep1, send1, keep2, send2 = wide_grads
            wide = jnp.concatenate(
                [reduce_path(keep1, send1, 4, 2), reduce_path(keep2, send2, 2, 4)], axis=0
            )
            extra = reduce_path(extra[:16], extra[16:], 4, 2)
            shards[layer] = (wide, extra[:ada_rows], extra[ada_rows, :bias_count])
        else:
            tail = jnp.pad(bias_rows[:, None], ((0, 0), (0, 0), (0, D - bias_count)))
            keep1, send1, keep2, send2 = wide_grads
            full = jnp.concatenate(
                [jnp.concatenate([keep1, send1], axis=0), jnp.concatenate([keep2, send2], axis=0)], axis=1
            )
            parts = [full[:, 48 * k : 48 * k + 48].reshape(size, attn_rows, D) for k in range(3)]
            parts = [part.astype(F32) for part in parts]
            packed = jnp.concatenate(parts + [ada_grad.reshape(size, ada_rows, D), tail], axis=1)
            total = lax.psum_scatter(packed, AXIS, scatter_dimension=0, tiled=False)
            shards[layer] = (
                total[: 3 * attn_rows],
                total[3 * attn_rows : 3 * attn_rows + ada_rows],
                total[-1, :bias_count],
            )
    cond_grad = cond_grad * silu_slope(cond_value)

    def stacked(pick):
        return jnp.stack([pick(shards[layer]) for layer in range(layers)])

    return (
        output,
        grad_latents,
        cond_grad,
        stacked(lambda s: s[1].T),
        stacked(lambda s: s[0][:attn_rows].T),
        stacked(lambda s: s[0][attn_rows : 2 * attn_rows].T),
        stacked(lambda s: s[0][2 * attn_rows :]),
        stacked(lambda s: s[2]),
    )


def solution(mesh):
    token = P("fsdp", None, None)
    column = P(None, None, "fsdp")
    row = P(None, "fsdp", None)
    return jax.shard_map(
        per_device,
        mesh=mesh,
        in_specs=(token, P("fsdp", None), P("fsdp"), column, column, column, row, P(None, "fsdp"), token),
        out_specs=(token, token, P("fsdp", None), column, column, column, row, P(None, "fsdp")),
        check_vma=False,
    )
```

```python
import jax
import jax.numpy as jnp
from jax import lax
from jax.experimental import pallas as pl
from jax.experimental.pallas import tpu as pltpu
from jax.sharding import PartitionSpec as P

HEADS = 6
D = 384
F = 1536
S = 256
BF = jnp.bfloat16
F32 = jnp.float32
SPLIT = 112
PAYLOAD = 224
BLOCKS = 32
ROWS = 144
AXIS = "fsdp"


def dot_nn(a, b):
    return lax.dot_general(a, b, (((1,), (0,)), ((), ())), preferred_element_type=F32)


def dot_nt(a, b):
    return lax.dot_general(a, b, (((1,), (1,)), ((), ())), preferred_element_type=F32)


def silu_value(v):
    return v / (1.0 + jnp.exp(-v))


def silu_slope(v):
    sigmoid = 1.0 / (1.0 + jnp.exp(-v))
    return sigmoid * (1.0 + v * (1.0 - sigmoid))


def layer_norm(v):
    centre = v - jnp.mean(v, -1, keepdims=True)
    spread = jnp.mean(centre * centre, -1, keepdims=True)
    inverse = lax.rsqrt(spread + 1e-06)
    return centre * inverse, inverse


def norm_back(e, y, inverse):
    first = jnp.mean(e, -1, keepdims=True)
    second = jnp.mean(e * y, -1, keepdims=True)
    return inverse * (e - first - y * second)


def gelu_parts(u):
    square = u * u
    tanh = jnp.tanh(u * (0.7978845608028654 + (0.7978845608028654 * 0.044715) * square))
    return square, tanh


def gelu_value(u):
    _, tanh = gelu_parts(u)
    half = 0.5 * u
    return half + half * tanh


def gelu_both(u):
    square, tanh = gelu_parts(u)
    half = 0.5 * u
    value = half + half * tanh
    inner = 0.7978845608028654 + (3 * 0.7978845608028654 * 0.044715) * square
    slope = 0.5 + 0.5 * tanh + half * (1.0 - tanh * tanh) * inner
    return value, slope


def stack_heads(pair):
    lane = lax.broadcasted_iota(jnp.int32, pair.shape, 1)
    zero = jnp.zeros_like(pair)
    return jnp.concatenate([jnp.where(lane < 64, pair, zero), jnp.where(lane >= 64, pair, zero)], axis=0)


def attn_weight_of(wv, low, high):
    return wv[low:high, 0:48, :].reshape((high - low) * 48, D)


def inner_chunk(wv, c, base):
    return wv[16 * c : 16 * c + 16, base : base + 48, :].reshape(768, D)


def tile_of(modulation, k):
    return modulation[:, k * D : (k + 1) * D]


def forward_body(r, mod, bias, wv, keep):
    qkv_ref, prob_ref, att_ref, br1_ref, mid_ref, inn_ref, br2_ref = keep
    normed, _ = layer_norm(r)
    hidden = (normed * (1.0 + tile_of(mod, 1)) + tile_of(mod, 0)).astype(BF)
    per = D // 48
    for part, at in ((0, 0), (1, None), (2, 1)):
        project = dot_nt(hidden, attn_weight_of(wv, part * per, part * per + per))
        if at is not None:
            project = project + tile_of(bias, at)
        qkv_ref[:, part * D : (part + 1) * D] = project.astype(BF)
    for pair in range(HEADS // 2):
        lo = pair * 128
        query = qkv_ref[:, lo : lo + 128] * jnp.asarray(0.125, BF)
        key = stack_heads(qkv_ref[:, D + lo : D + lo + 128])
        value = stack_heads(qkv_ref[:, 2 * D + lo : 2 * D + lo + 128])
        scores = dot_nt(query, key)
        for h in range(2):
            part = scores[:, h * S : (h + 1) * S]
            expo = jnp.exp(part - jnp.max(part, -1, keepdims=True))
            total = jnp.sum(expo, -1, keepdims=True)
            prob_ref[:, (2 * pair + h) * S : (2 * pair + h + 1) * S] = (expo * (1.0 / total)).astype(BF)
        probs = prob_ref[:, 2 * pair * S : (2 * pair + 2) * S]
        att_ref[:, lo : lo + 128] = dot_nn(probs, value).astype(BF)
    branch = dot_nt(att_ref[...], attn_weight_of(wv, 3 * per, 4 * per)) + tile_of(bias, 2)
    br1_ref[...] = branch
    middle = r + tile_of(mod, 2) * branch
    mid_ref[...] = middle
    normed, _ = layer_norm(middle)
    hidden = (normed * (1.0 + tile_of(mod, 4)) + tile_of(mod, 3)).astype(BF)
    branch = tile_of(bias, 3)
    for c in range(2):
        inner = dot_nt(hidden, inner_chunk(wv, c, 48)) + bias[:, 4 * D + 768 * c : 4 * D + 768 * (c + 1)]
        inn_ref[:, 768 * c : 768 * (c + 1)] = inner
        branch = branch + dot_nn(gelu_value(inner).astype(BF), inner_chunk(wv, c, 96))
    br2_ref[...] = branch
    return middle + tile_of(mod, 5) * branch


def column_sum(v):
    return jnp.sum(v, axis=0, keepdims=True)


def backward_body(g, r, mod, wv, keep, acc, dbias_ref, dmod_ref, row, dqkv_ref):
    qkv_ref, prob_ref, att_ref, br1_ref, mid_ref, inn_ref, br2_ref = keep
    acc_attn, acc_in, acc_out = acc
    per = D // 48

    def put(k, v):
        dmod_ref[pl.ds(row, 1), k * D : (k + 1) * D] = v

    def bias_add(lo, v):
        dbias_ref[:, lo : lo + v.shape[1]] += v

    d_br2 = (tile_of(mod, 5) * g).astype(BF)
    put(5, column_sum(g * br2_ref[...]))
    bias_add(3 * D, column_sum(d_br2.astype(F32)))
    d_br2_t = d_br2.T
    normed, inverse = layer_norm(mid_ref[...])
    scale = 1.0 + tile_of(mod, 4)
    hidden_t = (normed * scale + tile_of(mod, 3)).astype(BF).T
    d_hidden = None
    for c in range(2):
        cols = slice(768 * c, 768 * (c + 1))
        act, slope = gelu_both(inn_ref[:, cols])
        acc_out[:, cols] += dot_nn(d_br2_t, act.astype(BF))
        d_inner = (dot_nt(d_br2, inner_chunk(wv, c, 96)) * slope).astype(BF)
        bias_add(4 * D + 768 * c, column_sum(d_inner.astype(F32)))
        acc_in[:, cols] += dot_nn(hidden_t, d_inner)
        part = dot_nn(d_inner, inner_chunk(wv, c, 48))
        d_hidden = part if d_hidden is None else d_hidden + part
    put(4, column_sum(d_hidden * normed))
    put(3, column_sum(d_hidden))
    d_mid = g + norm_back(d_hidden * scale, normed, inverse)
    d_br1 = (tile_of(mod, 2) * d_mid).astype(BF)
    put(2, column_sum(d_mid * br1_ref[...]))
    bias_add(2 * D, column_sum(d_br1.astype(F32)))
    acc_attn[:, 3 * D : 4 * D] += dot_nn(att_ref[...].T, d_br1)
    d_att = dot_nn(d_br1, attn_weight_of(wv, 3 * per, 4 * per)).astype(BF)
    for pair in range(HEADS // 2):
        lo = pair * 128
        query = qkv_ref[:, lo : lo + 128] * jnp.asarray(0.125, BF)
        key = stack_heads(qkv_ref[:, D + lo : D + lo + 128])
        value = stack_heads(qkv_ref[:, 2 * D + lo : 2 * D + lo + 128])
        d_out = d_att[:, lo : lo + 128]
        both = d_out.astype(F32) * att_ref[:, lo : lo + 128].astype(F32)
        lane = lax.broadcasted_iota(jnp.int32, both.shape, 1)
        d_probs = dot_nt(d_out, value)
        pieces = []
        probs = []
        for h in range(2):
            chosen = lane < 64 if h == 0 else lane >= 64
            delta = jnp.sum(jnp.where(chosen, both, 0.0), -1, keepdims=True)
            prob = prob_ref[:, (2 * pair + h) * S : (2 * pair + h + 1) * S]
            probs.append(prob)
            pieces.append((prob.astype(F32) * (d_probs[:, h * S : (h + 1) * S] - delta)).astype(BF))
        d_query = (dot_nn(jnp.concatenate(pieces, axis=1), key) * 0.125).astype(BF)
        d_scores = jnp.concatenate(pieces, axis=0)
        d_key = dot_nn(split_rows(query.T), d_scores).T.astype(BF)
        d_value = dot_nn(split_rows(d_out.T), jnp.concatenate(probs, axis=0)).T.astype(BF)
        dqkv_ref[:, lo : lo + 128] = d_query
        dqkv_ref[:, D + lo : D + lo + 128] = d_key
        dqkv_ref[:, 2 * D + lo : 2 * D + lo + 128] = d_value
        bias_add(lo, column_sum(d_query.astype(F32)))
        bias_add(D + lo, column_sum(d_value.astype(F32)))
    normed, inverse = layer_norm(r)
    scale = 1.0 + tile_of(mod, 1)
    hidden_t = (normed * scale + tile_of(mod, 0)).astype(BF).T
    d_hidden = None
    for part in range(3):
        cols = slice(part * D, (part + 1) * D)
        d_part = dqkv_ref[:, cols]
        acc_attn[:, cols] += dot_nn(hidden_t, d_part)
        term = dot_nn(d_part, attn_weight_of(wv, part * per, part * per + per))
        d_hidden = term if d_hidden is None else d_hidden + term
    put(1, column_sum(d_hidden * normed))
    put(0, column_sum(d_hidden))
    return d_mid + norm_back(d_hidden * scale, normed, inverse)


def split_rows(pair):
    sub = lax.broadcasted_iota(jnp.int32, pair.shape, 0)
    zero = jnp.zeros_like(pair)
    return jnp.concatenate([jnp.where(sub < 64, pair, zero), jnp.where(sub >= 64, pair, zero)], axis=1)


def fetch_weights(table, pieces, wv, sem):
    copies = []
    for ref, (masks, low, rows) in pieces:
        for k, mask in enumerate(masks):
            block = table[mask]
            copies.append(
                pltpu.make_async_copy(
                    ref.at[k, pl.ds(0, rows), :], wv.at[block, pl.ds(low, rows), :], sem.at[len(copies)]
                )
            )
    for copy in copies:
        copy.start()
    for copy in copies:
        copy.wait()


def emit_grads(table, acc, stage, outs, orders, sem):
    for part, ref in enumerate(acc):
        for k in range(4):
            block = ref[:, k * D : (k + 1) * D].T.astype(BF)
            stage[8 * k : 8 * k + 8, 48 * part : 48 * part + 48, :] = block.reshape(8, 48, D)
    copies = []
    for ref, (masks, low, rows) in zip(outs, orders):
        for k, mask in enumerate(masks):
            copies.append(
                pltpu.make_async_copy(stage.at[table[mask], pl.ds(low, rows), :], ref.at[k], sem.at[len(copies)])
            )
    for copy in copies:
        copy.start()
    for copy in copies:
        copy.wait()


def saved_shapes():
    return [(3 * D, BF), (HEADS * S, BF), (D, BF), (D, F32), (D, F32), (F, F32), (D, F32)]


def run_forward(table, latents, mod, bias, pieces, layout):
    slots = latents.shape[0]
    count = len(pieces)

    def body(table_ref, lat_ref, mod_ref, bias_ref, *rest):
        piece_refs = rest[:count]
        keep = [ref.at[0] for ref in rest[count : count + 7]]
        out_ref, wv, sem = rest[count + 7 :]
        step = pl.program_id(0)

        @pl.when(step == 0)
        def _():
            fetch_weights(table_ref, list(zip(piece_refs, layout)), wv, sem)

        @pl.when(step < table_ref[BLOCKS])
        def _():
            out_ref[0] = forward_body(
                lat_ref[0].astype(F32), mod_ref[pl.ds(step, 1), :], bias_ref[...], wv, keep
            )

    clamp = lambda i, t: (jnp.minimum(i, t[BLOCKS] - 1), 0, 0)
    whole = lambda i, t: (0, 0)
    shapes = saved_shapes() + [(D, F32)]
    return pl.pallas_call(
        body,
        grid_spec=pltpu.PrefetchScalarGridSpec(
            num_scalar_prefetch=1,
            grid=(slots,),
            in_specs=[
                pl.BlockSpec((1, S, D), clamp),
                pl.BlockSpec(mod.shape, whole),
                pl.BlockSpec(bias.shape, whole),
            ]
            + [pl.BlockSpec(memory_space=pl.ANY)] * count,
            out_specs=[pl.BlockSpec((1, S, width), clamp) for width, _ in shapes],
            scratch_shapes=[
                pltpu.VMEM((32, ROWS, D), BF),
                pltpu.SemaphoreType.DMA((2 * BLOCKS,)),
            ],
        ),
        out_shape=[jax.ShapeDtypeStruct((slots, S, width), kind) for width, kind in shapes],
        cost_estimate=pl.CostEstimate(flops=slots * 1100000000, bytes_accessed=40000000, transcendentals=0),
        name="forward_zero",
    )(table, latents, mod, bias, *pieces)


def grad_outs():
    half = BLOCKS // 2
    shapes = [(half, SPLIT, D)] * 2 + [(half, ROWS - SPLIT, D)] * 2
    return [jax.ShapeDtypeStruct(shape, BF) for shape in shapes]


def run_middle(table, residual, cotangent, mod, bias, pieces, layout, orders):
    slots = residual.shape[0]
    count = len(pieces)

    def body(table_ref, res_ref, cot_ref, mod_ref, bias_ref, *rest):
        piece_refs = rest[:count]
        act_ref, g_ref, dmod_ref, dbias_ref = rest[count : count + 4]
        outs = rest[count + 4 : count + 8]
        wv, sem, a1, a2, a3, stage, dqkv = rest[count + 8 : count + 15]
        keep = rest[count + 15 :]
        acc = (a1, a2, a3)
        step = pl.program_id(0)

        @pl.when(step == 0)
        def _():
            fetch_weights(table_ref, list(zip(piece_refs, layout)), wv, sem)
            for ref in acc + (dbias_ref, dmod_ref):
                ref[...] = jnp.zeros_like(ref)

        @pl.when(step < table_ref[BLOCKS])
        def _():
            m = mod_ref[pl.ds(step, 1), :]
            r = res_ref[0]
            act_ref[0] = forward_body(r, m, bias_ref[...], wv, keep).astype(BF)
            g_ref[0] = backward_body(
                cot_ref[0].astype(F32), r, m, wv, keep, acc, dbias_ref, dmod_ref, step, dqkv
            )

        @pl.when(step >= table_ref[BLOCKS])
        def _():
            act_ref[0] = jnp.zeros((S, D), BF)

        @pl.when(step == slots - 1)
        def _():
            emit_grads(table_ref, acc, stage, outs, orders, sem)

    clamp = lambda i, t: (jnp.minimum(i, t[BLOCKS] - 1), 0, 0)
    each = lambda i, t: (i, 0, 0)
    whole = lambda i, t: (0, 0)
    any_spec = pl.BlockSpec(memory_space=pl.ANY)
    return pl.pallas_call(
        body,
        grid_spec=pltpu.PrefetchScalarGridSpec(
            num_scalar_prefetch=1,
            grid=(slots,),
            in_specs=[
                pl.BlockSpec((1, S, D), clamp),
                pl.BlockSpec((1, S, D), clamp),
                pl.BlockSpec(mod.shape, whole),
                pl.BlockSpec(bias.shape, whole),
            ]
            + [any_spec] * count,
            out_specs=[
                pl.BlockSpec((1, S, D), each),
                pl.BlockSpec((1, S, D), clamp),
                pl.BlockSpec((slots, 6 * D), whole),
                pl.BlockSpec((1, 8 * D), whole),
            ]
            + [any_spec] * 4,
            scratch_shapes=[
                pltpu.VMEM((32, ROWS, D), BF),
                pltpu.SemaphoreType.DMA((2 * BLOCKS,)),
                pltpu.VMEM((D, F), F32),
                pltpu.VMEM((D, F), F32),
                pltpu.VMEM((D, F), F32),
                pltpu.VMEM((32, ROWS, D), BF),
                pltpu.VMEM((S, 3 * D), BF),
            ]
            + [pltpu.VMEM((S, width), kind) for width, kind in saved_shapes()],
        ),
        out_shape=[
            jax.ShapeDtypeStruct((slots, S, D), BF),
            jax.ShapeDtypeStruct((slots, S, D), F32),
            jax.ShapeDtypeStruct((slots, 6 * D), F32),
            jax.ShapeDtypeStruct((1, 8 * D), F32),
        ]
        + grad_outs(),
        cost_estimate=pl.CostEstimate(flops=slots * 3300000000, bytes_accessed=20000000, transcendentals=0),
        name="middle_one",
    )(table, residual, cotangent, mod, bias, *pieces)


def run_backward(table, latents, upstream, mod, pieces, layout, saved, orders):
    slots = latents.shape[0]
    count = len(pieces)

    def body(table_ref, lat_ref, g_ref, mod_ref, *rest):
        keep = [ref.at[0] for ref in rest[:7]]
        piece_refs = rest[7 : 7 + count]
        rest = rest[7 + count :]
        out_ref, dmod_ref, dbias_ref = rest[:3]
        outs = rest[3:7]
        wv, sem, a1, a2, a3, stage, dqkv = rest[7:]
        acc = (a1, a2, a3)
        step = pl.program_id(0)

        @pl.when(step == 0)
        def _():
            fetch_weights(table_ref, list(zip(piece_refs, layout)), wv, sem)
            for ref in acc + (dbias_ref, dmod_ref):
                ref[...] = jnp.zeros_like(ref)

        @pl.when(step < table_ref[BLOCKS])
        def _():
            out_ref[0] = backward_body(
                g_ref[0],
                lat_ref[0].astype(F32),
                mod_ref[pl.ds(step, 1), :],
                wv,
                keep,
                acc,
                dbias_ref,
                dmod_ref,
                step,
                dqkv,
            )

        @pl.when(step >= table_ref[BLOCKS])
        def _():
            out_ref[0] = jnp.zeros((S, D), F32)

        @pl.when(step == slots - 1)
        def _():
            emit_grads(table_ref, acc, stage, outs, orders, sem)

    clamp = lambda i, t: (jnp.minimum(i, t[BLOCKS] - 1), 0, 0)
    each = lambda i, t: (i, 0, 0)
    whole = lambda i, t: (0, 0)
    any_spec = pl.BlockSpec(memory_space=pl.ANY)
    return pl.pallas_call(
        body,
        grid_spec=pltpu.PrefetchScalarGridSpec(
            num_scalar_prefetch=1,
            grid=(slots,),
            in_specs=[
                pl.BlockSpec((1, S, D), clamp),
                pl.BlockSpec((1, S, D), clamp),
                pl.BlockSpec(mod.shape, whole),
            ]
            + [pl.BlockSpec((1, S, width), clamp) for width, _ in saved_shapes()]
            + [any_spec] * count,
            out_specs=[
                pl.BlockSpec((1, S, D), each),
                pl.BlockSpec((slots, 6 * D), whole),
                pl.BlockSpec((1, 8 * D), whole),
            ]
            + [any_spec] * 4,
            scratch_shapes=[
                pltpu.VMEM((32, ROWS, D), BF),
                pltpu.SemaphoreType.DMA((2 * BLOCKS,)),
                pltpu.VMEM((D, F), F32),
                pltpu.VMEM((D, F), F32),
                pltpu.VMEM((D, F), F32),
                pltpu.VMEM((32, ROWS, D), BF),
                pltpu.VMEM((S, 3 * D), BF),
            ],
        ),
        out_shape=[
            jax.ShapeDtypeStruct((slots, S, D), F32),
            jax.ShapeDtypeStruct((slots, 6 * D), F32),
            jax.ShapeDtypeStruct((1, 8 * D), F32),
        ]
        + grad_outs(),
        cost_estimate=pl.CostEstimate(flops=slots * 2200000000, bytes_accessed=50000000, transcendentals=0),
        name="backward_zero",
    )(table, latents, upstream, mod, *saved, *pieces)


def permute(v, mask):
    size = lax.axis_size(AXIS)
    return lax.ppermute(v, AXIS, [(i, i ^ mask) for i in range(size)])


Z_MASKS = (0, 8, 16, 24)


def path_masks(first, second):
    order = [m for m in Z_MASKS]
    order = order + [m ^ second for m in order]
    return order + [m ^ first for m in order]


def tie(v, *after):
    return lax.optimization_barrier((v,) + after)[0]


def gather_line(shard):
    return jnp.stack([shard] + [permute(shard, m) for m in Z_MASKS[1:]])


def gather_near(line):
    one, two = line[:, :SPLIT], line[:, SPLIT:]
    near_one = jnp.concatenate([one, permute(one, 2)], axis=0)
    near_two = jnp.concatenate([two, permute(two, 4)], axis=0)
    return near_one, near_two


def gather_rest(near, far):
    return [near[0], far[0], permute(near[0], 1), permute(far[0], 1)], [
        near[1],
        far[1],
        permute(near[1], 1),
        permute(far[1], 1),
    ]


def gather_layout():
    layout = []
    for low, rows, masks in ((0, SPLIT, path_masks(4, 2)), (SPLIT, ROWS - SPLIT, path_masks(2, 4))):
        for core in (0, 1):
            for half in (0, 1):
                layout.append(([m ^ core for m in masks[8 * half : 8 * half + 8]], low, rows))
    return layout


def grad_orders():
    one, two = path_masks(4, 2), path_masks(2, 4)
    return [
        (one, 0, SPLIT),
        ([m ^ 1 for m in one], 0, SPLIT),
        (two, SPLIT, ROWS - SPLIT),
        ([m ^ 1 for m in two], SPLIT, ROWS - SPLIT),
    ]


def plain_layout():
    return [(list(range(BLOCKS)), 0, ROWS)]


def plain_orders():
    low, high = list(range(16)), list(range(16, 32))
    return [(low, 0, SPLIT), (high, 0, SPLIT), (low, SPLIT, ROWS - SPLIT), (high, SPLIT, ROWS - SPLIT)]


def added(*terms):
    total = terms[0].astype(F32)
    for term in terms[1:]:
        total = total + term.astype(F32)
    return total


def reduce_core(wide_grads, extra):
    keep1, send1, keep2, send2 = wide_grads
    keep2 = jnp.concatenate([keep2, extra[:16]], axis=1)
    send2 = jnp.concatenate([send2, extra[16:]], axis=1)
    return added(keep1, permute(send1, 1)).astype(BF), added(keep2, permute(send2, 1)).astype(BF)


def reduce_rest(one, two):
    one = added(one[:8], permute(one[8:], 4)).astype(BF)
    two = added(two[:8], permute(two[8:], 2)).astype(BF)
    one = added(one[:4], permute(one[4:], 2)).astype(BF)
    two = added(two[:4], permute(two[4:], 4)).astype(BF)
    both = jnp.concatenate([one, two], axis=1)
    return added(both[0], *[permute(both[k], Z_MASKS[k]) for k in range(1, 4)])


def rank_matrix(me):
    masks = path_masks(2, 4)
    masks = jnp.asarray(masks + [m ^ 1 for m in masks], jnp.int32)
    return (masks[None, :] ^ me) == jnp.arange(BLOCKS, dtype=jnp.int32)[:, None]


def per_device(
    latents, cond, live_counts, ada_weight, attn_weight, mlp_in, mlp_out, bias_all, cotangent
):
    slots = latents.shape[0]
    layers = ada_weight.shape[0]
    fast = lax.axis_size(AXIS) == BLOCKS
    size = lax.axis_size(AXIS)
    me = lax.axis_index(AXIS)
    order = jnp.arange(BLOCKS, dtype=jnp.int32)
    if fast:
        order = order ^ me
    table = jnp.concatenate([order, live_counts.astype(jnp.int32)])
    cond_value = cond.astype(F32)
    cond_low = silu_value(cond_value).astype(BF)
    ada_rows = ada_weight.shape[2]
    attn_rows = attn_weight.shape[2]
    bias_count = bias_all.shape[1]
    layout = gather_layout() if fast else plain_layout()
    orders = grad_orders() if fast else plain_orders()
    rank = rank_matrix(me) if fast else None

    def payload(layer):
        bias_row = jnp.pad(bias_all[layer], (0, D - bias_count))[None]
        if fast:
            bias_row = jnp.pad(bias_row, ((0, 7), (0, 0)))
        parts = [attn_weight[layer].T, mlp_in[layer].T, mlp_out[layer], ada_weight[layer].T, bias_row]
        return jnp.concatenate(parts, axis=0)

    def modulation(ada, bias):
        bias = bias.reshape(-1).astype(F32)
        modulate = jnp.einsum("sd,jed->sje", cond_low, ada, preferred_element_type=F32)
        if fast:
            modulate = jnp.einsum(
                "jp,spe->sje", rank.astype(F32), modulate, precision=lax.Precision.HIGHEST
            )
        return bias[None, 6 * D :], modulate.reshape(slots, 6 * D) + bias[: 6 * D]

    def unpack_fast(one, two):
        full = jnp.concatenate([p[:, ROWS - SPLIT :] for p in two], axis=0)
        ada = full[:, :ada_rows]
        bias = jnp.dot(rank.astype(BF), full[:, ada_rows, :bias_count], preferred_element_type=F32)
        return (one + two, ada) + modulation(ada, bias)

    def unpack_plain(full):
        parts = [full[:, k * attn_rows : (k + 1) * attn_rows].reshape(BLOCKS, 48, D) for k in range(3)]
        ada = full[:, 3 * attn_rows : 3 * attn_rows + ada_rows].reshape(BLOCKS, -1, D)
        bias = full[:, 3 * attn_rows + ada_rows, :bias_count]
        return ([jnp.concatenate(parts, axis=1)], ada) + modulation(ada, bias)

    def local_grads(layer, result, ada):
        grad_modulate, grad_bias = result[:2]
        grad_low = grad_modulate.astype(BF)
        bias_full = jnp.concatenate([jnp.sum(grad_low.astype(F32), axis=0), grad_bias[0]])
        grouped = grad_low.reshape(slots, BLOCKS, -1)
        bias_rows = bias_full.reshape(size, bias_count).astype(BF)
        if fast:
            grouped = jnp.einsum(
                "jp,sje->spe", rank.astype(BF), grouped, preferred_element_type=F32
            ).astype(BF)
            bias_rows = jnp.einsum("jp,je->pe", rank.astype(BF), bias_rows, preferred_element_type=F32)
        cond_part = jnp.einsum("sje,jed->sd", grouped, ada, preferred_element_type=F32)
        ada_grad = jnp.einsum("sje,sd->jed", grouped, cond_low, preferred_element_type=F32)
        tail = jnp.pad(bias_rows[:, None], ((0, 0), (0, 7 if fast else 0), (0, D - bias_count)))
        if fast:
            return cond_part, jnp.concatenate([ada_grad.astype(BF), tail.astype(BF)], axis=1)
        keep1, send1, keep2, send2 = result[2:]
        full = jnp.concatenate(
            [jnp.concatenate([keep1, send1], axis=0), jnp.concatenate([keep2, send2], axis=0)], axis=1
        )
        parts = [full[:, 48 * k : 48 * k + 48].reshape(size, attn_rows, D).astype(F32) for k in range(3)]
        parts = parts + [ada_grad.reshape(size, ada_rows, D), tail.astype(F32)]
        return cond_part, jnp.concatenate(parts, axis=1)

    cond_grad = jnp.zeros(cond_value.shape, F32)
    shards = [None] * layers
    if fast:
        line0 = gather_line(payload(0))
        line1 = gather_line(tie(payload(1), line0))
        near0 = gather_near(line0)
        far0 = (permute(near0[0], 4), permute(near0[1], 2))
        near1 = gather_near(tie(line1, *far0))
        block0 = unpack_fast(*gather_rest(near0, far0))
        far1 = (permute(near1[0], 4), permute(near1[1], 2))
        first_table = tie(table, *near1)
    else:
        full = [lax.all_gather(payload(layer), AXIS, axis=0, tiled=False) for layer in range(layers)]
        block0 = unpack_plain(full[0])
        first_table = table
    saved = run_forward(first_table, latents, block0[3], block0[2], block0[0], layout)
    if fast:
        block1 = unpack_fast(*gather_rest(near1, far1))
    else:
        block1 = unpack_plain(full[1])
    middle = run_middle(
        table, saved[7], cotangent, block1[3], block1[2], block1[0], layout, orders
    )
    output, upstream = middle[:2]
    cond_part, extra = local_grads(1, middle[2:], block1[1])
    cond_grad = cond_grad + cond_part
    last_table = table
    if fast:
        one1, two1 = reduce_core(middle[4:], extra)
        last_table = tie(table, one1, two1)
    else:
        shards[1] = lax.psum_scatter(extra, AXIS, scatter_dimension=0, tiled=False)
    last = run_backward(
        last_table, latents, upstream, block0[3], block0[0], layout, saved[:7], orders
    )
    grad_latents = last[0]
    cond_part, extra = local_grads(0, last[1:], block0[1])
    cond_grad = cond_grad + cond_part
    if fast:
        one0, two0 = reduce_core(last[3:], extra)
        shards[1] = reduce_rest(one1, two1)
        shards[0] = reduce_rest(one0, two0)
    else:
        shards[0] = lax.psum_scatter(extra, AXIS, scatter_dimension=0, tiled=False)
    cond_grad = cond_grad * silu_slope(cond_value)

    def stacked(pick):
        return jnp.stack([pick(shards[layer]) for layer in range(layers)])

    wide = 3 * attn_rows
    return (
        output,
        grad_latents,
        cond_grad,
        stacked(lambda s: s[wide : wide + ada_rows].T),
        stacked(lambda s: s[:attn_rows].T),
        stacked(lambda s: s[attn_rows : 2 * attn_rows].T),
        stacked(lambda s: s[2 * attn_rows : wide]),
        stacked(lambda s: s[wide + ada_rows, :bias_count]),
    )


def solution(mesh):
    token = P("fsdp", None, None)
    column = P(None, None, "fsdp")
    row = P(None, "fsdp", None)
    return jax.shard_map(
        per_device,
        mesh=mesh,
        in_specs=(token, P("fsdp", None), P("fsdp"), column, column, column, row, P(None, "fsdp"), token),
        out_specs=(token, token, P("fsdp", None), column, column, column, row, P(None, "fsdp")),
        check_vma=False,
    )
```

```python
import jax
import jax.numpy as jnp
from jax import lax
from jax.experimental import pallas as pl
from jax.experimental.pallas import tpu as pltpu
from jax.sharding import PartitionSpec as P


HEADS = 6
D = 384
F = 1536
S = 256
BF = jnp.bfloat16
F32 = jnp.float32
SPLIT = 112
BLOCKS = 32
ROWS = 144
AXIS = "fsdp"


def dot_nn(a, b):
    return lax.dot_general(a, b, (((1,), (0,)), ((), ())), preferred_element_type=F32)


def dot_nt(a, b):
    return lax.dot_general(a, b, (((1,), (1,)), ((), ())), preferred_element_type=F32)


def silu_value(v):
    return v / (1.0 + jnp.exp(-v))


def silu_slope(v):
    sigmoid = 1.0 / (1.0 + jnp.exp(-v))
    return sigmoid * (1.0 + v * (1.0 - sigmoid))


def layer_norm(v):
    centre = v - jnp.mean(v, -1, keepdims=True)
    spread = jnp.mean(centre * centre, -1, keepdims=True)
    inverse = lax.rsqrt(spread + 1e-06)
    return centre * inverse, inverse


def norm_back(e, y, inverse):
    first = jnp.mean(e, -1, keepdims=True)
    second = jnp.mean(e * y, -1, keepdims=True)
    return inverse * (e - first - y * second)


def gelu_parts(u):
    square = u * u
    tanh = jnp.tanh(u * (0.7978845608028654 + (0.7978845608028654 * 0.044715) * square))
    return square, tanh


def gelu_value(u):
    _, tanh = gelu_parts(u)
    half = 0.5 * u
    return half + half * tanh


def gelu_both(u):
    square, tanh = gelu_parts(u)
    half = 0.5 * u
    value = half + half * tanh
    inner = 0.7978845608028654 + (3 * 0.7978845608028654 * 0.044715) * square
    slope = 0.5 + 0.5 * tanh + half * (1.0 - tanh * tanh) * inner
    return value, slope


def stack_heads(pair):
    lane = lax.broadcasted_iota(jnp.int32, pair.shape, 1)
    zero = jnp.zeros_like(pair)
    return jnp.concatenate([jnp.where(lane < 64, pair, zero), jnp.where(lane >= 64, pair, zero)], axis=0)


def attn_weight_of(wv, low, high):
    return wv[low:high, 0:48, :].reshape((high - low) * 48, D)


def inner_chunk(wv, c, base):
    return wv[16 * c : 16 * c + 16, base : base + 48, :].reshape(768, D)


def tile_of(modulation, k):
    return modulation[:, k * D : (k + 1) * D]


def forward_body(r, mod, bias, wv, keep):
    qkv_ref, prob_ref, att_ref, br1_ref, mid_ref, inn_ref, br2_ref = keep
    normed, _ = layer_norm(r)
    hidden = (normed * (1.0 + tile_of(mod, 1)) + tile_of(mod, 0)).astype(BF)
    per = D // 48
    for part, at in ((0, 0), (1, None), (2, 1)):
        project = dot_nt(hidden, attn_weight_of(wv, part * per, part * per + per))
        if at is not None:
            project = project + tile_of(bias, at)
        qkv_ref[:, part * D : (part + 1) * D] = project.astype(BF)
    for pair in range(HEADS // 2):
        lo = pair * 128
        query = qkv_ref[:, lo : lo + 128] * jnp.asarray(0.125, BF)
        key = stack_heads(qkv_ref[:, D + lo : D + lo + 128])
        value = stack_heads(qkv_ref[:, 2 * D + lo : 2 * D + lo + 128])
        scores = dot_nt(query, key)
        for h in range(2):
            part = scores[:, h * S : (h + 1) * S]
            expo = jnp.exp(part - jnp.max(part, -1, keepdims=True))
            total = jnp.sum(expo, -1, keepdims=True)
            prob_ref[:, (2 * pair + h) * S : (2 * pair + h + 1) * S] = (expo * (1.0 / total)).astype(BF)
        probs = prob_ref[:, 2 * pair * S : (2 * pair + 2) * S]
        att_ref[:, lo : lo + 128] = dot_nn(probs, value).astype(BF)
    branch = dot_nt(att_ref[...], attn_weight_of(wv, 3 * per, 4 * per)) + tile_of(bias, 2)
    br1_ref[...] = branch
    middle = r + tile_of(mod, 2) * branch
    mid_ref[...] = middle
    normed, _ = layer_norm(middle)
    hidden = (normed * (1.0 + tile_of(mod, 4)) + tile_of(mod, 3)).astype(BF)
    branch = tile_of(bias, 3)
    for c in range(2):
        inner = dot_nt(hidden, inner_chunk(wv, c, 48)) + bias[:, 4 * D + 768 * c : 4 * D + 768 * (c + 1)]
        inn_ref[:, 768 * c : 768 * (c + 1)] = inner
        branch = branch + dot_nn(gelu_value(inner).astype(BF), inner_chunk(wv, c, 96))
    br2_ref[...] = branch
    return middle + tile_of(mod, 5) * branch


def column_sum(v):
    return jnp.sum(v, axis=0, keepdims=True)


def backward_body(g, r, mod, wv, keep, acc, dbias_ref, dmod_ref, row, dqkv_ref):
    qkv_ref, prob_ref, att_ref, br1_ref, mid_ref, inn_ref, br2_ref = keep
    acc_attn, acc_in, acc_out = acc
    per = D // 48

    def put(k, v):
        dmod_ref[pl.ds(row, 1), k * D : (k + 1) * D] = v

    def bias_add(lo, v):
        dbias_ref[:, lo : lo + v.shape[1]] += v

    d_br2 = (tile_of(mod, 5) * g).astype(BF)
    put(5, column_sum(g * br2_ref[...]))
    bias_add(3 * D, column_sum(d_br2.astype(F32)))
    d_br2_t = d_br2.T
    normed, inverse = layer_norm(mid_ref[...])
    scale = 1.0 + tile_of(mod, 4)
    hidden_t = (normed * scale + tile_of(mod, 3)).astype(BF).T
    d_hidden = None
    for c in range(2):
        cols = slice(768 * c, 768 * (c + 1))
        act, slope = gelu_both(inn_ref[:, cols])
        acc_out[:, cols] += dot_nn(d_br2_t, act.astype(BF))
        d_inner = (dot_nt(d_br2, inner_chunk(wv, c, 96)) * slope).astype(BF)
        bias_add(4 * D + 768 * c, column_sum(d_inner.astype(F32)))
        acc_in[:, cols] += dot_nn(hidden_t, d_inner)
        part = dot_nn(d_inner, inner_chunk(wv, c, 48))
        d_hidden = part if d_hidden is None else d_hidden + part
    put(4, column_sum(d_hidden * normed))
    put(3, column_sum(d_hidden))
    d_mid = g + norm_back(d_hidden * scale, normed, inverse)
    d_br1 = (tile_of(mod, 2) * d_mid).astype(BF)
    put(2, column_sum(d_mid * br1_ref[...]))
    bias_add(2 * D, column_sum(d_br1.astype(F32)))
    acc_attn[:, 3 * D : 4 * D] += dot_nn(att_ref[...].T, d_br1)
    d_att = dot_nn(d_br1, attn_weight_of(wv, 3 * per, 4 * per)).astype(BF)
    for pair in range(HEADS // 2):
        lo = pair * 128
        query = qkv_ref[:, lo : lo + 128] * jnp.asarray(0.125, BF)
        key = stack_heads(qkv_ref[:, D + lo : D + lo + 128])
        value = stack_heads(qkv_ref[:, 2 * D + lo : 2 * D + lo + 128])
        d_out = d_att[:, lo : lo + 128]
        both = d_out.astype(F32) * att_ref[:, lo : lo + 128].astype(F32)
        lane = lax.broadcasted_iota(jnp.int32, both.shape, 1)
        d_probs = dot_nt(d_out, value)
        pieces = []
        probs = []
        for h in range(2):
            chosen = lane < 64 if h == 0 else lane >= 64
            delta = jnp.sum(jnp.where(chosen, both, 0.0), -1, keepdims=True)
            prob = prob_ref[:, (2 * pair + h) * S : (2 * pair + h + 1) * S]
            probs.append(prob)
            pieces.append((prob.astype(F32) * (d_probs[:, h * S : (h + 1) * S] - delta)).astype(BF))
        d_query = (dot_nn(jnp.concatenate(pieces, axis=1), key) * 0.125).astype(BF)
        d_scores = jnp.concatenate(pieces, axis=0)
        d_key = dot_nn(split_rows(query.T), d_scores).T.astype(BF)
        d_value = dot_nn(split_rows(d_out.T), jnp.concatenate(probs, axis=0)).T.astype(BF)
        dqkv_ref[:, lo : lo + 128] = d_query
        dqkv_ref[:, D + lo : D + lo + 128] = d_key
        dqkv_ref[:, 2 * D + lo : 2 * D + lo + 128] = d_value
        bias_add(lo, column_sum(d_query.astype(F32)))
        bias_add(D + lo, column_sum(d_value.astype(F32)))
    normed, inverse = layer_norm(r)
    scale = 1.0 + tile_of(mod, 1)
    hidden_t = (normed * scale + tile_of(mod, 0)).astype(BF).T
    d_hidden = None
    for part in range(3):
        cols = slice(part * D, (part + 1) * D)
        d_part = dqkv_ref[:, cols]
        acc_attn[:, cols] += dot_nn(hidden_t, d_part)
        term = dot_nn(d_part, attn_weight_of(wv, part * per, part * per + per))
        d_hidden = term if d_hidden is None else d_hidden + term
    put(1, column_sum(d_hidden * normed))
    put(0, column_sum(d_hidden))
    return d_mid + norm_back(d_hidden * scale, normed, inverse)


def split_rows(pair):
    sub = lax.broadcasted_iota(jnp.int32, pair.shape, 0)
    zero = jnp.zeros_like(pair)
    return jnp.concatenate([jnp.where(sub < 64, pair, zero), jnp.where(sub >= 64, pair, zero)], axis=1)


def fetch_weights(table, pieces, wv, sem, clear=()):
    copies = []
    for ref, (masks, low, rows) in pieces:
        for k, mask in enumerate(masks):
            block = table[mask]
            copies.append(
                pltpu.make_async_copy(
                    ref.at[k, pl.ds(0, rows), :], wv.at[block, pl.ds(low, rows), :], sem.at[len(copies)]
                )
            )
    for copy in copies:
        copy.start()
    for ref in clear:
        ref[...] = jnp.zeros_like(ref)
    for copy in copies:
        copy.wait()


def emit_grads(table, acc, stage, outs, orders, sem):
    for part, ref in enumerate(acc):
        for k in range(4):
            block = ref[:, k * D : (k + 1) * D].T.astype(BF)
            stage[8 * k : 8 * k + 8, 48 * part : 48 * part + 48, :] = block.reshape(8, 48, D)
    copies = []
    for ref, (masks, low, rows) in zip(outs, orders):
        for k, mask in enumerate(masks):
            copies.append(
                pltpu.make_async_copy(stage.at[table[mask], pl.ds(low, rows), :], ref.at[k], sem.at[len(copies)])
            )
    for copy in copies:
        copy.start()
    for copy in copies:
        copy.wait()


def saved_shapes():
    return [(3 * D, BF), (HEADS * S, BF), (D, BF), (D, F32), (D, F32), (F, F32), (D, F32)]


def run_forward(table, latents, mod, bias, pieces, layout):
    slots = latents.shape[0]
    count = len(pieces)

    def body(table_ref, lat_ref, mod_ref, bias_ref, *rest):
        piece_refs = rest[:count]
        keep = [ref.at[0] for ref in rest[count : count + 7]]
        out_ref, wv, sem = rest[count + 7 :]
        step = pl.program_id(0)

        @pl.when(step == 0)
        def _():
            fetch_weights(table_ref, list(zip(piece_refs, layout)), wv, sem)

        @pl.when(step < table_ref[BLOCKS])
        def _():
            out_ref[0] = forward_body(
                lat_ref[0].astype(F32), mod_ref[pl.ds(step, 1), :], bias_ref[...], wv, keep
            )

    clamp = lambda i, t: (jnp.minimum(i, t[BLOCKS] - 1), 0, 0)
    whole = lambda i, t: (0, 0)
    shapes = saved_shapes() + [(D, F32)]
    return pl.pallas_call(
        body,
        grid_spec=pltpu.PrefetchScalarGridSpec(
            num_scalar_prefetch=1,
            grid=(slots,),
            in_specs=[
                pl.BlockSpec((1, S, D), clamp),
                pl.BlockSpec(mod.shape, whole),
                pl.BlockSpec(bias.shape, whole),
            ]
            + [pl.BlockSpec(memory_space=pl.ANY)] * count,
            out_specs=[pl.BlockSpec((1, S, width), clamp) for width, _ in shapes],
            scratch_shapes=[
                pltpu.VMEM((32, ROWS, D), BF),
                pltpu.SemaphoreType.DMA((2 * BLOCKS,)),
            ],
        ),
        out_shape=[jax.ShapeDtypeStruct((slots, S, width), kind) for width, kind in shapes],
        cost_estimate=pl.CostEstimate(flops=slots * 1100000000, bytes_accessed=40000000, transcendentals=0),
        name="forward_zero",
    )(table, latents, mod, bias, *pieces)


def grad_outs():
    half = BLOCKS // 2
    shapes = [(half, SPLIT, D)] * 2 + [(half, ROWS - SPLIT, D)] * 2
    return [jax.ShapeDtypeStruct(shape, BF) for shape in shapes]


def run_middle(table, residual, cotangent, mod, bias, pieces, layout, orders):
    slots = residual.shape[0]
    count = len(pieces)

    def body(table_ref, res_ref, cot_ref, mod_ref, bias_ref, *rest):
        piece_refs = rest[:count]
        act_ref, g_ref, dmod_ref, dbias_ref = rest[count : count + 4]
        outs = rest[count + 4 : count + 8]
        wv, sem, a1, a2, a3, stage, dqkv = rest[count + 8 : count + 15]
        keep = rest[count + 15 :]
        acc = (a1, a2, a3)
        step = pl.program_id(0)

        @pl.when(step == 0)
        def _():
            fetch_weights(table_ref, list(zip(piece_refs, layout)), wv, sem, acc + (dbias_ref, dmod_ref))

        @pl.when(step < table_ref[BLOCKS])
        def _():
            m = mod_ref[pl.ds(step, 1), :]
            r = res_ref[0]
            act_ref[0] = forward_body(r, m, bias_ref[...], wv, keep).astype(BF)
            g_ref[0] = backward_body(
                cot_ref[0].astype(F32), r, m, wv, keep, acc, dbias_ref, dmod_ref, step, dqkv
            )

        @pl.when(step >= table_ref[BLOCKS])
        def _():
            act_ref[0] = jnp.zeros((S, D), BF)

        @pl.when(step == slots - 1)
        def _():
            emit_grads(table_ref, acc, stage, outs, orders, sem)

    clamp = lambda i, t: (jnp.minimum(i, t[BLOCKS] - 1), 0, 0)
    each = lambda i, t: (i, 0, 0)
    whole = lambda i, t: (0, 0)
    any_spec = pl.BlockSpec(memory_space=pl.ANY)
    return pl.pallas_call(
        body,
        grid_spec=pltpu.PrefetchScalarGridSpec(
            num_scalar_prefetch=1,
            grid=(slots,),
            in_specs=[
                pl.BlockSpec((1, S, D), clamp),
                pl.BlockSpec((1, S, D), clamp),
                pl.BlockSpec(mod.shape, whole),
                pl.BlockSpec(bias.shape, whole),
            ]
            + [any_spec] * count,
            out_specs=[
                pl.BlockSpec((1, S, D), each),
                pl.BlockSpec((1, S, D), clamp),
                pl.BlockSpec((slots, 6 * D), whole),
                pl.BlockSpec((1, 8 * D), whole),
            ]
            + [any_spec] * 4,
            scratch_shapes=[
                pltpu.VMEM((32, ROWS, D), BF),
                pltpu.SemaphoreType.DMA((2 * BLOCKS,)),
                pltpu.VMEM((D, F), F32),
                pltpu.VMEM((D, F), F32),
                pltpu.VMEM((D, F), F32),
                pltpu.VMEM((32, ROWS, D), BF),
                pltpu.VMEM((S, 3 * D), BF),
            ]
            + [pltpu.VMEM((S, width), kind) for width, kind in saved_shapes()],
        ),
        out_shape=[
            jax.ShapeDtypeStruct((slots, S, D), BF),
            jax.ShapeDtypeStruct((slots, S, D), F32),
            jax.ShapeDtypeStruct((slots, 6 * D), F32),
            jax.ShapeDtypeStruct((1, 8 * D), F32),
        ]
        + grad_outs(),
        cost_estimate=pl.CostEstimate(flops=slots * 3300000000, bytes_accessed=20000000, transcendentals=0),
        name="middle_one",
    )(table, residual, cotangent, mod, bias, *pieces)


def run_backward(table, latents, upstream, mod, pieces, layout, saved, orders):
    slots = latents.shape[0]
    count = len(pieces)

    def body(table_ref, lat_ref, g_ref, mod_ref, *rest):
        keep = [ref.at[0] for ref in rest[:7]]
        piece_refs = rest[7 : 7 + count]
        rest = rest[7 + count :]
        out_ref, dmod_ref, dbias_ref = rest[:3]
        outs = rest[3:7]
        wv, sem, a1, a2, a3, stage, dqkv = rest[7:]
        acc = (a1, a2, a3)
        step = pl.program_id(0)

        @pl.when(step == 0)
        def _():
            fetch_weights(table_ref, list(zip(piece_refs, layout)), wv, sem, acc + (dbias_ref, dmod_ref))

        @pl.when(step < table_ref[BLOCKS])
        def _():
            out_ref[0] = backward_body(
                g_ref[0],
                lat_ref[0].astype(F32),
                mod_ref[pl.ds(step, 1), :],
                wv,
                keep,
                acc,
                dbias_ref,
                dmod_ref,
                step,
                dqkv,
            )

        @pl.when(step >= table_ref[BLOCKS])
        def _():
            out_ref[0] = jnp.zeros((S, D), F32)

        @pl.when(step == slots - 1)
        def _():
            emit_grads(table_ref, acc, stage, outs, orders, sem)

    clamp = lambda i, t: (jnp.minimum(i, t[BLOCKS] - 1), 0, 0)
    each = lambda i, t: (i, 0, 0)
    whole = lambda i, t: (0, 0)
    any_spec = pl.BlockSpec(memory_space=pl.ANY)
    return pl.pallas_call(
        body,
        grid_spec=pltpu.PrefetchScalarGridSpec(
            num_scalar_prefetch=1,
            grid=(slots,),
            in_specs=[
                pl.BlockSpec((1, S, D), clamp),
                pl.BlockSpec((1, S, D), clamp),
                pl.BlockSpec(mod.shape, whole),
            ]
            + [pl.BlockSpec((1, S, width), clamp) for width, _ in saved_shapes()]
            + [any_spec] * count,
            out_specs=[
                pl.BlockSpec((1, S, D), each),
                pl.BlockSpec((slots, 6 * D), whole),
                pl.BlockSpec((1, 8 * D), whole),
            ]
            + [any_spec] * 4,
            scratch_shapes=[
                pltpu.VMEM((32, ROWS, D), BF),
                pltpu.SemaphoreType.DMA((2 * BLOCKS,)),
                pltpu.VMEM((D, F), F32),
                pltpu.VMEM((D, F), F32),
                pltpu.VMEM((D, F), F32),
                pltpu.VMEM((32, ROWS, D), BF),
                pltpu.VMEM((S, 3 * D), BF),
            ],
        ),
        out_shape=[
            jax.ShapeDtypeStruct((slots, S, D), F32),
            jax.ShapeDtypeStruct((slots, 6 * D), F32),
            jax.ShapeDtypeStruct((1, 8 * D), F32),
        ]
        + grad_outs(),
        cost_estimate=pl.CostEstimate(flops=slots * 2200000000, bytes_accessed=50000000, transcendentals=0),
        name="backward_zero",
    )(table, latents, upstream, mod, *saved, *pieces)


def permute(v, mask):
    size = lax.axis_size(AXIS)
    return lax.ppermute(v, AXIS, [(i, i ^ mask) for i in range(size)])


Z_MASKS = (0, 8, 16, 24)


def path_masks(first, second):
    order = [m for m in Z_MASKS]
    order = order + [m ^ second for m in order]
    return order + [m ^ first for m in order]


def tie(v, *after):
    return lax.optimization_barrier((v,) + after)[0]


def gather_line(shard):
    return jnp.stack([shard] + [permute(shard, m) for m in Z_MASKS[1:]])


def gather_near(line):
    one, two = line[:, :SPLIT], line[:, SPLIT:]
    near_one = jnp.concatenate([one, permute(one, 2)], axis=0)
    near_two = jnp.concatenate([two, permute(two, 4)], axis=0)
    return near_one, near_two


def gather_rest(near, far):
    return [near[0], far[0], permute(near[0], 1), permute(far[0], 1)], [
        near[1],
        far[1],
        permute(near[1], 1),
        permute(far[1], 1),
    ]


def gather_layout():
    layout = []
    for low, rows, masks in ((0, SPLIT, path_masks(4, 2)), (SPLIT, ROWS - SPLIT, path_masks(2, 4))):
        for core in (0, 1):
            for half in (0, 1):
                layout.append(([m ^ core for m in masks[8 * half : 8 * half + 8]], low, rows))
    return layout


def grad_orders():
    one, two = path_masks(4, 2), path_masks(2, 4)
    return [
        (one, 0, SPLIT),
        ([m ^ 1 for m in one], 0, SPLIT),
        (two, SPLIT, ROWS - SPLIT),
        ([m ^ 1 for m in two], SPLIT, ROWS - SPLIT),
    ]


def plain_layout():
    return [(list(range(BLOCKS)), 0, ROWS)]


def plain_orders():
    low, high = list(range(16)), list(range(16, 32))
    return [(low, 0, SPLIT), (high, 0, SPLIT), (low, SPLIT, ROWS - SPLIT), (high, SPLIT, ROWS - SPLIT)]


def added(*terms):
    total = terms[0].astype(F32)
    for term in terms[1:]:
        total = total + term.astype(F32)
    return total


def reduce_core(wide_grads, extra):
    keep1, send1, keep2, send2 = wide_grads
    keep2 = jnp.concatenate([keep2, extra[:16]], axis=1)
    send2 = jnp.concatenate([send2, extra[16:]], axis=1)
    return added(keep1, permute(send1, 1)).astype(BF), added(keep2, permute(send2, 1)).astype(BF)


def reduce_near(one, two):
    from_one = permute(one[8:], 4)
    from_two = permute(two[8:], 2)
    return from_one, from_two


def reduce_rest(one, two, near):
    one = added(one[:8], near[0]).astype(BF)
    two = added(two[:8], near[1]).astype(BF)
    one = added(one[:4], permute(one[4:], 2)).astype(BF)
    two = added(two[:4], permute(two[4:], 4)).astype(BF)
    both = jnp.concatenate([one, two], axis=1)
    return added(both[0], *[permute(both[k], Z_MASKS[k]) for k in range(1, 4)])


def rank_matrix(me):
    masks = path_masks(2, 4)
    masks = jnp.asarray(masks + [m ^ 1 for m in masks], jnp.int32)
    return (masks[None, :] ^ me) == jnp.arange(BLOCKS, dtype=jnp.int32)[:, None]


def whole_step(
    latents, cond, live_counts, ada_weight, attn_weight, mlp_in, mlp_out, bias_all, cotangent
):
    slots = latents.shape[0]
    layers = ada_weight.shape[0]
    fast = lax.axis_size(AXIS) == BLOCKS
    size = lax.axis_size(AXIS)
    me = lax.axis_index(AXIS)
    order = jnp.arange(BLOCKS, dtype=jnp.int32)
    if fast:
        order = order ^ me
    table = jnp.concatenate([order, live_counts.astype(jnp.int32)])
    cond_value = cond.astype(F32)
    cond_low = silu_value(cond_value).astype(BF)
    ada_rows = ada_weight.shape[2]
    attn_rows = attn_weight.shape[2]
    bias_count = bias_all.shape[1]
    layout = gather_layout() if fast else plain_layout()
    orders = grad_orders() if fast else plain_orders()
    rank = rank_matrix(me) if fast else None

    def payload(layer):
        bias_row = jnp.pad(bias_all[layer], (0, D - bias_count))[None]
        if fast:
            bias_row = jnp.pad(bias_row, ((0, 7), (0, 0)))
        parts = [attn_weight[layer].T, mlp_in[layer].T, mlp_out[layer], ada_weight[layer].T, bias_row]
        return jnp.concatenate(parts, axis=0)

    def modulation(ada, bias):
        bias = bias.reshape(-1).astype(F32)
        modulate = [
            jnp.einsum("sd,jed->sje", cond_low, part, preferred_element_type=F32) for part in ada
        ]
        modulate = jnp.concatenate(modulate, axis=1)
        if fast:
            modulate = jnp.einsum(
                "jp,spe->sje", rank.astype(F32), modulate, precision=lax.Precision.HIGHEST
            )
        return bias[None, 6 * D :], modulate.reshape(slots, 6 * D) + bias[: 6 * D]

    def unpack_fast(one, two):
        base = ROWS - SPLIT
        ada = [p[:, base : base + ada_rows] for p in two]
        bias = jnp.concatenate([p[:, base + ada_rows, :bias_count] for p in two], axis=0)
        bias = jnp.dot(rank.astype(BF), bias, preferred_element_type=F32)
        return (one + two, ada) + modulation(ada, bias)

    def unpack_plain(full):
        parts = [full[:, k * attn_rows : (k + 1) * attn_rows].reshape(BLOCKS, 48, D) for k in range(3)]
        ada = [full[:, 3 * attn_rows : 3 * attn_rows + ada_rows].reshape(BLOCKS, -1, D)]
        bias = full[:, 3 * attn_rows + ada_rows, :bias_count]
        return ([jnp.concatenate(parts, axis=1)], ada) + modulation(ada, bias)

    def local_grads(result, ada):
        grad_modulate, grad_bias = result[:2]
        grad_low = grad_modulate.astype(BF)
        bias_full = jnp.concatenate([jnp.sum(grad_low.astype(F32), axis=0), grad_bias[0]])
        grouped = grad_low.reshape(slots, BLOCKS, -1)
        bias_rows = bias_full.reshape(size, bias_count).astype(BF)
        if fast:
            grouped = jnp.einsum(
                "jp,sje->spe", rank.astype(BF), grouped, preferred_element_type=F32
            ).astype(BF)
            bias_rows = jnp.einsum("jp,je->pe", rank.astype(BF), bias_rows, preferred_element_type=F32)
        cond_part = 0.0
        for k, part in enumerate(ada):
            chunk = grouped[:, k * part.shape[0] : (k + 1) * part.shape[0]]
            cond_part = cond_part + jnp.einsum("sje,jed->sd", chunk, part, preferred_element_type=F32)
        ada_grad = jnp.einsum("sje,sd->jed", grouped, cond_low, preferred_element_type=F32)
        tail = jnp.pad(bias_rows[:, None], ((0, 0), (0, 7 if fast else 0), (0, D - bias_count)))
        if fast:
            return cond_part, jnp.concatenate([ada_grad.astype(BF), tail.astype(BF)], axis=1)
        keep1, send1, keep2, send2 = result[2:]
        full = jnp.concatenate(
            [jnp.concatenate([keep1, send1], axis=0), jnp.concatenate([keep2, send2], axis=0)], axis=1
        )
        parts = [full[:, 48 * k : 48 * k + 48].reshape(size, attn_rows, D).astype(F32) for k in range(3)]
        parts = parts + [ada_grad.reshape(size, ada_rows, D), tail.astype(F32)]
        return cond_part, jnp.concatenate(parts, axis=1)

    cond_grad = jnp.zeros(cond_value.shape, F32)
    shards = [None] * layers
    if fast:
        line0 = gather_line(payload(0))
        line1 = gather_line(tie(payload(1), line0))
        near0 = gather_near(line0)
        far0 = (permute(near0[0], 4), permute(near0[1], 2))
        near1 = gather_near(tie(line1, *far0))
        block0 = unpack_fast(*gather_rest(near0, far0))
        far_one = permute(near1[0], 4)
        far_two = permute(near1[1], 2)
        far1 = (far_one, far_two)
        first_table = tie(table, *near1)
    else:
        full = [lax.all_gather(payload(layer), AXIS, axis=0, tiled=False) for layer in range(layers)]
        block0 = unpack_plain(full[0])
        first_table = table
    saved = run_forward(first_table, latents, block0[3], block0[2], block0[0], layout)
    if fast:
        block1 = unpack_fast(*gather_rest(near1, far1))
    else:
        block1 = unpack_plain(full[1])
    middle = run_middle(
        table, saved[7], cotangent, block1[3], block1[2], block1[0], layout, orders
    )
    output, upstream = middle[:2]
    cond_part, extra = local_grads(middle[2:], block1[1])
    cond_grad = cond_grad + cond_part
    last_table = table
    if fast:
        one1, two1 = reduce_core(middle[4:], extra)
        last_table = tie(table, one1, two1)
        reduced1 = reduce_near(one1, two1)
    else:
        shards[1] = lax.psum_scatter(extra, AXIS, scatter_dimension=0, tiled=False)
    last = run_backward(
        last_table, latents, upstream, block0[3], block0[0], layout, saved[:7], orders
    )
    grad_latents = last[0]
    cond_part, extra = local_grads(last[1:], block0[1])
    cond_grad = cond_grad + cond_part
    if fast:
        one0, two0 = reduce_core(last[3:], extra)
        shards[1] = reduce_rest(one1, two1, reduced1)
        shards[0] = reduce_rest(one0, two0, reduce_near(one0, two0))
    else:
        shards[0] = lax.psum_scatter(extra, AXIS, scatter_dimension=0, tiled=False)
    cond_grad = cond_grad * silu_slope(cond_value)

    def stacked(pick):
        return jnp.stack([pick(shards[layer]) for layer in range(layers)])

    wide = 3 * attn_rows
    return (
        output,
        grad_latents,
        cond_grad,
        stacked(lambda s: s[wide : wide + ada_rows].T),
        stacked(lambda s: s[:attn_rows].T),
        stacked(lambda s: s[attn_rows : 2 * attn_rows].T),
        stacked(lambda s: s[2 * attn_rows : wide]),
        stacked(lambda s: s[wide + ada_rows, :bias_count]),
    )


def solution(mesh):
    token = P("fsdp", None, None)
    column = P(None, None, "fsdp")
    row = P(None, "fsdp", None)
    return jax.shard_map(
        whole_step,
        mesh=mesh,
        in_specs=(token, P("fsdp", None), P("fsdp"), column, column, column, row, P(None, "fsdp"), token),
        out_specs=(token, token, P("fsdp", None), column, column, column, row, P(None, "fsdp")),
        check_vma=False,
    )
```
